256 devices in a mesh: gx: 32 (over z_hi, x, y), gy: 8 (over z_lo, core).
Axes of the slice: x: 4, y: 4, z: 8 (z_hi: 2, z_lo: 4; z = z_hi * 4 + z_lo), core: 2. Of those that a mesh axis runs over, the one named last changes fastest.
Arguments:
- motion: float32 [3, 64, 96, 1024], P(None, 'gx', None, 'gy'), may hold values from -6 to 6
- stress: float32 [6, 64, 96, 1024], P(None, 'gx', None, 'gy'), may hold values from -6 to 6
- buoyancy: float32 [64, 96, 1024], P('gx', None, 'gy'), may hold values from 0.5 to 1.5
- lame_first: float32 [64, 96, 1024], P('gx', None, 'gy'), may hold values from 0.5 to 1.5
- lame_shear: float32 [64, 96, 1024], P('gx', None, 'gy'), may hold values from 0.5 to 1.5
- surface: float32 [512, 8192], P('gx', 'gy'), may hold values from -2 to 2
- momentum: float32 [2, 512, 8192], P(None, 'gx', 'gy'), may hold values from -3 to 3
- bathymetry: float32 [512, 8192], P('gx', 'gy'), may hold values from 2 to 4
- wet_mask: int32 [512, 8192], P('gx', 'gy'), may hold values 0 or 1
Outputs:
- final_motion: float32 [3, 64, 96, 1024], P(None, 'gx', None, 'gy')
- final_stress: float32 [6, 64, 96, 1024], P(None, 'gx', None, 'gy')
- final_surface: float32 [512, 8192], P('gx', 'gy')
- final_momentum: float32 [2, 512, 8192], P(None, 'gx', 'gy')
The draws below stay inside these ranges and needn't reach their ends.
Inputs may be any that keep to these rules, and one draw needn't show every extreme that they name: `wet_mask`: 1 marks a wet ocean cell, 0 a dry one.
All inputs are finite; a program needn't handle non-finite values. No bound on the sum of `wet_mask` on one device may be relied on, other than what follows from the above.
Results may differ from the reference program's by a relative error of at most 0.0001.
Values sent between devices are 32-bit elements; how exact they have to be, the bound alone decides.
No kernel may reach another device: no remote copies, remote signals or barrier semaphores. Data moves between devices by JAX's collectives and lax.ppermute only.
A program may use at most 64 MiB of HBM per device.

```python
import jax
import jax.numpy as jnp

SX = 2
Z = 96
RATIO = 8
STEPS = 4
NSUB = 4
NXS = 64
NYS = 1024
NXO = 512
NYO = 8192


def touch_ends(result, key, least, high):
    extent = result.shape
    place = [jax.random.randint(jax.random.fold_in(key, axis), (), 0, extent[axis]) for axis in range(len(extent))]
    result = result.at[tuple(place)].set(least)
    longest = extent.index(max(extent))
    place[longest] = (place[longest] + 1) % extent[longest]
    return result.at[tuple(place)].set(high)


def steps_of(own_key, dims, cuts, least, high):
    level, own = 1.0, jax.random.fold_in(own_key, 6)
    for axis_at, blocks in cuts:
        heights = jnp.exp(jax.random.uniform(jax.random.fold_in(own, axis_at), (blocks,), jnp.float32, least / len(cuts), high / len(cuts)))
        level = level * jnp.repeat(heights, dims[axis_at] // blocks).reshape([-1 if axis == axis_at else 1 for axis in range(len(dims))])
    return level


def gaussian(stream_key, extent, width, most, shards=(), held_as=jnp.bfloat16):
    result = width * jax.random.normal(stream_key, extent, jnp.float32)
    if shards:
        result = result * steps_of(stream_key, extent, shards, -0.22, 0.18)
    return jnp.clip(result, -most, most).astype(held_as)


def setup_inputs(seed: int = 0) -> dict:
    seeds = jax.random.split(jax.random.key(seed), 10)
    return {
        "motion": gaussian(seeds[0], (3, NXS, Z, NYS), 1.0, 6.0, ((1, 32), (3, 8)), jnp.float32),
        "stress": gaussian(seeds[1], (6, NXS, Z, NYS), 1.0, 6.0, ((1, 32), (3, 8)), jnp.float32),
        "buoyancy": jnp.clip(0.5 + 1.0 * jax.random.uniform(seeds[2], (NXS, Z, NYS), jnp.float32) ** steps_of(seeds[2], (NXS, Z, NYS), ((0, 32), (2, 8)), -0.2, 0.2), 0.5, 1.5),
        "lame_first": jnp.clip(0.5 + 1.0 * jax.random.uniform(seeds[3], (NXS, Z, NYS), jnp.float32) ** steps_of(seeds[3], (NXS, Z, NYS), ((0, 32), (2, 8)), -0.2, 0.2), 0.5, 1.5),
        "lame_shear": jnp.clip(0.5 + 1.0 * jax.random.uniform(seeds[4], (NXS, Z, NYS), jnp.float32) ** steps_of(seeds[4], (NXS, Z, NYS), ((0, 32), (2, 8)), -0.2, 0.2), 0.5, 1.5),
        "surface": gaussian(seeds[5], (NXO, NYO), 0.25, 2.0, ((0, 32), (1, 8)), jnp.float32),
        "momentum": gaussian(seeds[6], (2, NXO, NYO), 0.5, 3.0, ((1, 32), (2, 8)), jnp.float32),
        "bathymetry": jnp.clip(2.0 + 2.0 * jax.random.uniform(seeds[7], (NXO, NYO), jnp.float32) ** steps_of(seeds[7], (NXO, NYO), ((0, 32), (1, 8)), -0.2, 0.2), 2.0, 4.0),
        "wet_mask": touch_ends((jax.random.randint(seeds[8], (NXO, NYO), 0, 8) < 7).astype(jnp.int32), jax.random.fold_in(seeds[8], 1), 0, 1),
    }


SOLID_STEP = 0.2
WAVE_STEP = 0.1
VISCOSITY = 0.05
UPLIFT_GAIN = 0.25
LOAD_GAIN = 8.0


def middle(quantity):
    return quantity[1:-1, :, 1:-1]


def ahead_x(quantity):
    return quantity[2:, :, 1:-1]


def behind_x(quantity):
    return quantity[:-2, :, 1:-1]


def ahead_y(quantity):
    return quantity[1:-1, :, 2:]


def behind_y(quantity):
    return quantity[1:-1, :, :-2]


def ahead_z(quantity):
    return jnp.concatenate([quantity[:, 1:], jnp.zeros_like(quantity[:, :1])], axis=1)


def behind_z(quantity):
    return jnp.concatenate([jnp.zeros_like(quantity[:, :1]), quantity[:, :-1]], axis=1)


def advance_velocity(motion, stress, buoyancy):
    stress_xx, stress_yy, stress_zz = stress[0], stress[1], stress[2]
    stress_xy, stress_xz, stress_yz = stress[3], stress[4], stress[5]
    mid_xy = middle(stress_xy)
    mid_xz = middle(stress_xz)
    mid_yz = middle(stress_yz)
    mid_zz = middle(stress_zz)
    step_rate = SOLID_STEP * buoyancy
    force_x = (ahead_x(stress_xx) - middle(stress_xx)) + (mid_xy - behind_y(stress_xy)) + (mid_xz - behind_z(mid_xz))
    force_y = (mid_xy - behind_x(stress_xy)) + (ahead_y(stress_yy) - middle(stress_yy)) + (mid_yz - behind_z(mid_yz))
    force_z = (mid_xz - behind_x(stress_xz)) + (mid_yz - behind_y(stress_yz)) + (ahead_z(mid_zz) - mid_zz)
    return jnp.stack([motion[0] + step_rate * force_x, motion[1] + step_rate * force_y, motion[2] + step_rate * force_z])


def advance_stress(stress, motion, lame_first, lame_shear):
    speed_x, speed_y, speed_z = motion[0], motion[1], motion[2]
    centre_x = middle(speed_x)
    centre_y = middle(speed_y)
    centre_z = middle(speed_z)
    strain_x = centre_x - behind_x(speed_x)
    strain_y = centre_y - behind_y(speed_y)
    strain_z = centre_z - behind_z(centre_z)
    stiffness = lame_first + 2.0 * lame_shear
    normal_xx = stress[0] + SOLID_STEP * (stiffness * strain_x + lame_first * (strain_y + strain_z))
    normal_yy = stress[1] + SOLID_STEP * (stiffness * strain_y + lame_first * (strain_x + strain_z))
    normal_zz = stress[2] + SOLID_STEP * (stiffness * strain_z + lame_first * (strain_x + strain_y))
    shear_rate = SOLID_STEP * lame_shear
    shear_xy = stress[3] + shear_rate * ((ahead_y(speed_x) - centre_x) + (ahead_x(speed_y) - centre_y))
    shear_xz = stress[4] + shear_rate * ((ahead_z(centre_x) - centre_x) + (ahead_x(speed_z) - centre_z))
    shear_yz = stress[5] + shear_rate * ((ahead_z(centre_y) - centre_y) + (ahead_y(speed_z) - centre_z))
    return jnp.stack([normal_xx, normal_yy, normal_zz, shear_xy, shear_xz, shear_yz])


def apply_load(stress, seafloor_load):
    return stress.at[2, :, 0, :].set(-LOAD_GAIN * seafloor_load)


def interior(quantity):
    return quantity[1:-1, 1:-1]


def wave_substep(ocean_state, seabed):
    height, flow_x, flow_y = ocean_state[0], ocean_state[1], ocean_state[2]
    depth_in = seabed[0, 1:-1, 1:-1]
    wet_full = seabed[1]
    wet_in = wet_full[1:-1, 1:-1]
    extent_x, extent_y = height.shape
    height_new = height[1:, 1:] - WAVE_STEP * wet_in[1:, 1:] * ((flow_x[1:, 1:] - flow_x[:-1, 1:]) + (flow_y[1:, 1:] - flow_y[1:, :-1]))
    centre = height_new[:-1, :-1]
    east_side = height_new[1:, :-1]
    north_side = height_new[:-1, 1:]
    face_x = wet_full[:-1, :] * wet_full[1:, :]
    face_y = wet_full[:, :-1] * wet_full[:, 1:]
    flow_cx = interior(flow_x)
    spread_x = (face_x[3:extent_x + 1, 2:extent_y] * (flow_x[2:, 1:-1] - flow_cx)
                + face_x[1:extent_x - 1, 2:extent_y] * (flow_x[:-2, 1:-1] - flow_cx)
                + face_x[2:extent_x, 3:extent_y + 1] * (flow_x[1:-1, 2:] - flow_cx)
                + face_x[2:extent_x, 1:extent_y - 1] * (flow_x[1:-1, :-2] - flow_cx))
    flow_cy = interior(flow_y)
    spread_y = (face_y[3:extent_x + 1, 2:extent_y] * (flow_y[2:, 1:-1] - flow_cy)
                + face_y[1:extent_x - 1, 2:extent_y] * (flow_y[:-2, 1:-1] - flow_cy)
                + face_y[2:extent_x, 3:extent_y + 1] * (flow_y[1:-1, 2:] - flow_cy)
                + face_y[2:extent_x, 1:extent_y - 1] * (flow_y[1:-1, :-2] - flow_cy))
    depth_c = interior(depth_in)
    depth_east = depth_in[2:, 1:-1]
    depth_north = depth_in[1:-1, 2:]
    new_flow_x = face_x[2:extent_x, 2:extent_y] * (flow_cx - WAVE_STEP * 0.5 * (depth_c + depth_east + centre + east_side) * (east_side - centre) + VISCOSITY * spread_x)
    new_flow_y = face_y[2:extent_x, 2:extent_y] * (flow_cy - WAVE_STEP * 0.5 * (depth_c + depth_north + centre + north_side) * (north_side - centre) + VISCOSITY * spread_y)
    return jnp.stack([centre, new_flow_x, new_flow_y])


def upsample(coarse):
    count_x, count_y = coarse.shape
    spread_out = jnp.broadcast_to(coarse[:, None, :, None], (count_x, RATIO, count_y, RATIO))
    return spread_out.reshape(count_x * RATIO, count_y * RATIO)


def block_average(fine_grid):
    count_x, count_y = fine_grid.shape
    return jnp.mean(fine_grid.reshape(count_x // RATIO, RATIO, count_y // RATIO, RATIO), axis=(1, 3))


def reference(motion, stress, buoyancy, lame_first, lame_shear, surface, momentum, bathymetry, wet_mask):
    wet_float = wet_mask.astype(jnp.float32)
    seabed = jnp.pad(jnp.stack([bathymetry, wet_float]), ((0, 0), (2, 2), (2, 2)))
    ocean_state = jnp.concatenate([surface[None], momentum], axis=0)
    half_rows = SX // 2
    count_x = motion.shape[1]
    count_y = motion.shape[3]
    zero_rows = jnp.zeros((half_rows, count_y), jnp.float32)
    for coupling_step in range(STEPS):
        top_speed = motion[2, :, 0, :]
        uplift = jnp.concatenate([zero_rows, top_speed[:count_x - half_rows]], axis=0)
        lifted = ocean_state[0] + UPLIFT_GAIN * wet_float * upsample(uplift)
        ocean_state = ocean_state.at[0].set(lifted)
        for substep in range(NSUB):
            padded = jnp.pad(ocean_state, ((0, 0), (1, 1), (1, 1)))
            ocean_state = wave_substep(padded, seabed)
        averaged = block_average(wet_float * ocean_state[0])
        seafloor_load = jnp.concatenate([averaged[half_rows:], zero_rows], axis=0)
        stress_padded = jnp.pad(stress, ((0, 0), (1, 1), (0, 0), (1, 1)))
        motion = advance_velocity(motion, stress_padded, buoyancy)
        motion_padded = jnp.pad(motion, ((0, 0), (1, 1), (0, 0), (1, 1)))
        stress = advance_stress(stress, motion_padded, lame_first, lame_shear)
        stress = apply_load(stress, seafloor_load)
    return motion, stress, ocean_state[0], ocean_state[1:]
```

```python
import functools

import jax
import jax.numpy as jnp
from jax import lax
from jax.experimental import pallas as pl
from jax.experimental.pallas import tpu as pltpu
from jax.sharding import PartitionSpec as P

STEPS = 4
NSUB = 4
SOLID_STEP = 0.2
WAVE_STEP = 0.1
VISCOSITY = 0.05
UPLIFT_GAIN = 0.25
LOAD_GAIN = 8.0

INTERPRET = False
LANES = 128
TILES = 9
OCEAN = 3 * TILES * 8


def iota(shape, dim):
    return lax.broadcasted_iota(jnp.int32, shape, dim)


def roll(value, shift, axis):
    shift = shift % value.shape[axis]
    return value if shift == 0 else pltpu.roll(value, shift, axis)


def prev_lane(value):
    return roll(value, 1, 1)


def next_lane(value):
    return roll(value, -1, 1)


def below(get, k):
    current = roll(get(k), 1, 0)
    other = roll(get(k - 1), 1, 0) if k > 0 else jnp.zeros_like(current)
    return jnp.where(iota(current.shape, 0) == 0, other, current)


def above(get, k, slabs):
    current = roll(get(k), -1, 0)
    other = roll(get(k + 1), -1, 0) if k < slabs - 1 else jnp.zeros_like(current)
    return jnp.where(iota(current.shape, 0) == 7, other, current)


def expander():
    shape = (LANES, LANES)
    return jnp.where(iota(shape, 0) == iota(shape, 1) >> 3, 1.0, 0.0)


def reducer():
    shape = (LANES, LANES)
    return jnp.where(iota(shape, 0) >> 3 == iota(shape, 1), 1.0 / 64.0, 0.0)


def exact_dot(left, right):
    return jnp.dot(
        left, right, precision=lax.Precision.HIGHEST, preferred_element_type=jnp.float32
    )


def upsampled(rows):
    lane, line = iota((8, LANES), 1), iota((8, LANES), 0)
    stack = []
    for row in rows:
        own = jnp.broadcast_to(row[:, :LANES], (8, LANES))
        halo = jnp.broadcast_to(row[:, LANES:], (8, LANES))
        tiles = own
        for t in range(1, 8):
            tiles = jnp.where(line == t, roll(own, -16 * t, 1), tiles)
        stack += [tiles, jnp.where(lane < 4, halo, roll(halo, 16, 1))]
    spread = exact_dot(jnp.concatenate(stack, axis=0), expander())
    return [spread[16 * i : 16 * i + 16] for i in range(len(rows))]


def block_means(sums):
    lane, line = iota((8, LANES), 1), iota((8, LANES), 0)
    stack = []
    for tiles in sums:
        wide = [jnp.broadcast_to(tile, (8, LANES)) for tile in tiles]
        own = wide[0]
        for t in range(1, 8):
            own = jnp.where(line == t, wide[t], own)
        stack += [own, wide[8]]
    mean = exact_dot(jnp.concatenate(stack, axis=0), reducer())
    rows = []
    for i in range(len(sums)):
        tiles, last = mean[16 * i : 16 * i + 8], mean[16 * i + 8 : 16 * i + 16]
        own = jnp.zeros((8, LANES), jnp.float32)
        for t in range(8):
            own = jnp.where((line == t) & (lane >> 4 == t), roll(tiles, 16 * t, 1), own)
        own = jnp.sum(own, axis=0, keepdims=True)
        halo = jnp.where(lane < 4, last, jnp.where(lane >= 124, roll(last, 112, 1), 0.0))
        rows.append(jnp.concatenate([own, halo[0:1]], axis=1))
    return rows


class Sender:
    def __init__(self, even, first_ref, second_ref):
        self.even, self.first, self.second = even, first_ref, second_ref

    def put(self, at, right, left):
        end = at + right.shape[0]
        self.first[at:end, :] = jnp.where(self.even, right, left)
        self.second[at:end, :] = jnp.where(self.even, left, right)

    def put_solid(self, at, slabs, right, left):
        lane = iota((8, LANES), 1)
        tails = [jnp.zeros((8, LANES), jnp.float32) for _ in range(2)]
        for k in range(slabs):
            here = (lane >= 8 * k) & (lane < 8 * k + 8)
            values = (right(k), left(k))
            for i, value in enumerate(values):
                tails[i] = jnp.where(here, roll(value[:, LANES:], 4 + 8 * k, 1), tails[i])
            self.put(at + 8 * k, values[0][:, :LANES], values[1][:, :LANES])
        self.put(at + 8 * slabs, *tails)


class Receiver:
    def __init__(self, even, first_ref, second_ref):
        self.even, self.first, self.second = even, first_ref, second_ref

    def right(self, at):
        return jnp.where(self.even, self.first[at : at + 8, :], self.second[at : at + 8, :])

    def left(self, at):
        return jnp.where(self.even, self.second[at : at + 8, :], self.first[at : at + 8, :])

    def solid(self, side, at, k, slabs):
        take = self.right if side > 0 else self.left
        tail = roll(take(at + 8 * slabs), -(4 + 8 * k), 1)
        return jnp.concatenate([take(at + 8 * k), tail], axis=1)


def offsets(slabs):
    part = 8 * slabs + 8
    ocean = 3 * part
    extra = ocean + OCEAN
    more = extra + 16
    return part, ocean, extra, more, more + part


def payload_rows(slabs, kind):
    part, _, _, more, static = offsets(slabs)
    return {"first": static + 4 * TILES * 8, "usual": more, "last": more + OCEAN}[kind]


def finish(out, slabs, motion, stress, buoyancy, ocean, wet, mean_row, kind, static=None):
    part, ocean_at, extra_at, more_at, static_at = offsets(slabs)

    def get(ref, field, row):
        return lambda k: ref[field, row, 8 * k : 8 * k + 8, :]

    def rate(row, k):
        return SOLID_STEP * buoyancy[0, row, 8 * k : 8 * k + 8, :]

    def sum_x(k):
        xx, xy, xz = (get(stress, f, 1) for f in (0, 3, 4))
        mid = xy(k)
        force = (mid - prev_lane(mid)) + (xz(k) - below(xz, k)) - xx(k)
        return get(motion, 0, 1)(k) + rate(1, k) * force

    def sum_y(k):
        xy, yy, yz = (get(stress, f, 0) for f in (3, 1, 5))
        mid = yy(k)
        force = xy(k) + (next_lane(mid) - mid) + (yz(k) - below(yz, k))
        return get(motion, 1, 0)(k) + rate(0, k) * force

    def sum_z(k):
        xz, yz, zz = (get(stress, f, 0) for f in (4, 5, 2))
        mid = yz(k)
        force = xz(k) + (mid - prev_lane(mid)) + (above(zz, k, slabs) - zz(k))
        return get(motion, 2, 0)(k) + rate(0, k) * force

    out.put_solid(0, slabs, sum_x, sum_y)
    out.put_solid(part, slabs, get(stress, 3, 1), sum_z)
    out.put_solid(2 * part, slabs, get(stress, 4, 1), get(stress, 0, 0))
    (spread,) = upsampled([motion[2, 0, 0:1, :]])
    for t in range(TILES):
        ocean[0, t, 8:16, :] = (
            ocean[0, t, 8:16, :] + UPLIFT_GAIN * wet[t, 8:16, :] * spread[t : t + 1]
        )
        for f in range(3):
            at = (f * TILES + t) * 8
            lower, upper = ocean[f, t, 0:8, :], ocean[f, t, 8:16, :]
            out.put(ocean_at + at, upper, lower)
            if kind == "last":
                out.put(more_at + at, upper, upper)
    top = motion[2, 1, 0:8, :]
    mean_row = jnp.zeros((8, 256), jnp.float32) if mean_row is None else mean_row
    mean_row = jnp.broadcast_to(mean_row, (8, 256))
    for i in range(2):
        lanes = slice(LANES * i, LANES * i + LANES)
        out.put(extra_at + 8 * i, top[:, lanes], mean_row[:, lanes])
    if kind == "first":
        out.put_solid(more_at, slabs, get(buoyancy, 0, 1), get(buoyancy, 0, 0))
        for f, array in enumerate(static):
            for t in range(TILES):
                at = static_at + (f * 2 * TILES + t) * 8
                lower, upper = array[t, 0:8, :], array[t, 8:16, :]
                out.put(at, upper, lower)
                out.put(at + TILES * 8, upper, upper)


def pack_y_kernel(
    parity, motion, stress, buoyancy, first, shear, surface, momentum, depth, wet, one, two
):
    even = parity[1] == 0
    out = Sender(even, one, two)
    slabs = motion.shape[2] // 8
    lane = iota((8, LANES), 1)
    fields = [(motion, f) for f in range(3)] + [(stress, f) for f in range(6)]
    fields += [(buoyancy, None), (first, None), (shear, None)]
    count, at = 0, 0
    right = left = jnp.zeros((8, LANES), jnp.float32)
    for ref, f in fields:
        for row in range(2):
            for k in range(slabs):
                z = slice(8 * k, 8 * k + 8)
                value = ref[row, z, :] if f is None else ref[f, row, z, :]
                here = lane >> 2 == count
                right = jnp.where(here, roll(value, 4 * count + 4, 1), right)
                left = jnp.where(here, roll(value, 4 * count, 1), left)
                count += 1
                if count == 32:
                    out.put(at, right, left)
                    count, at = 0, at + 8
    if count:
        out.put(at, right, left)
        count, at = 0, at + 8
    width = surface.shape[1]
    for ref, f in ((surface, None), (momentum, 0), (momentum, 1), (depth, None), (wet, None)):
        for group in range(2):
            rows = slice(8 * group, 8 * group + 8)
            ends = []
            for lanes in (slice(0, LANES), slice(width - LANES, width)):
                value = ref[rows, lanes] if f is None else ref[f, rows, lanes]
                ends.append(value.astype(jnp.float32))
            here = lane >> 5 == count
            right = jnp.where(here, roll(ends[1], 32 * count + 32, 1), right)
            left = jnp.where(here, roll(ends[0], 32 * count, 1), left)
            count += 1
            if count == 4:
                out.put(at, right, left)
                count, at = 0, at + 8
    if count:
        out.put(at, right, left)


def pack_y_rows(slabs):
    return 8 * (-(-24 * slabs // 32) + 3)


def start_kernel(
    parity, motion, stress, buoyancy, first, shear, surface, momentum, depth, wet, one, two,
    motion_out, stress_out, solid_out, ocean_out, floor_out, send_one, send_two,
):
    inbox = Receiver(parity[1] == 0, one, two)
    slabs = motion.shape[2] // 8
    lane = iota((8, LANES), 1)
    fields = [(motion, f, motion_out, f) for f in range(3)]
    fields += [(stress, f, stress_out, f) for f in range(6)]
    fields += [(ref, None, solid_out, f) for f, ref in enumerate((buoyancy, first, shear))]
    count, at = 0, 0
    for ref, f, target, g in fields:
        for row in range(2):
            for k in range(slabs):
                z = slice(8 * k, 8 * k + 8)
                value = ref[row, z, :] if f is None else ref[f, row, z, :]
                if count == 0:
                    packed = inbox.right(at), inbox.left(at)
                after = roll(packed[0], -4 * count, 1)
                before = roll(packed[1], 124 - 4 * count, 1)
                halo = jnp.where(lane < 4, after, jnp.where(lane >= 124, before, 0.0))
                target[g, row, z, 0:LANES] = value
                target[g, row, z, LANES : 2 * LANES] = halo
                count += 1
                if count == 32:
                    count, at = 0, at + 8
    if count:
        count, at = 0, at + 8
    targets = ((surface, None), (momentum, 0), (momentum, 1), (depth, None), (wet, None))
    for i, (ref, f) in enumerate(targets):
        for group in range(2):
            rows = slice(8 * group, 8 * group + 8)
            if count == 0:
                packed = inbox.right(at), inbox.left(at)
            after = roll(packed[0], -32 * count, 1)
            before = roll(packed[1], 96 - 32 * count, 1)
            halo = jnp.where(lane < 32, after, jnp.where(lane >= 96, before, 0.0))
            for t in range(TILES):
                if t == TILES - 1:
                    value = halo
                else:
                    lanes = slice(LANES * t, LANES * t + LANES)
                    value = ref[rows, lanes] if f is None else ref[f, rows, lanes]
                    value = value.astype(jnp.float32)
                if i < 3:
                    ocean_out[i, t, rows, :] = value
                else:
                    floor_out[i - 3, t, rows, :] = value
            count += 1
            if count == 4:
                count, at = 0, at + 8
    out = Sender(parity[0] == 0, send_one, send_two)
    static = (floor_out.at[0], floor_out.at[1])
    finish(
        out, slabs, motion_out, stress_out, solid_out, ocean_out, floor_out.at[1], None, "first",
        static,
    )


def ocean_part(
    inbox, base, slabs, motion, ocean, floor, kind, coef, height, flow, row_left
):
    _, ocean_at, _, more_at, static_at = offsets(slabs)
    wide = kind == "last"
    low = iota((8, LANES), 0) < 4

    def joined(upper, lower):
        return jnp.where(low, upper, lower)

    def floor_tile(f, t, wide_rows):
        at = static_at + (f * 2 * TILES + t) * 8
        near, far, top = base.right(at), base.right(at + TILES * 8), base.left(at)
        own = floor[f, t, :, :]
        if wide_rows:
            return jnp.concatenate([own, near, joined(far, top)], axis=0)
        return jnp.concatenate([own, joined(near, top)], axis=0)

    def narrowed(value):
        if wide:
            return value
        return jnp.concatenate([value[0:16], joined(value[16:24], value[24:32])], axis=0)

    lane0 = lambda rows: iota((rows, LANES), 1) == 0
    lane127 = lambda rows: iota((rows, LANES), 1) == LANES - 1

    def west(tile, t):
        mine, other = roll(tile(t), 1, 1), roll(tile((t - 1) % TILES), 1, 1)
        return jnp.where(lane0(mine.shape[0]), other, mine)

    def east(tile, t):
        mine, other = roll(tile(t), -1, 1), roll(tile((t + 1) % TILES), -1, 1)
        return jnp.where(lane127(mine.shape[0]), other, mine)

    own_last = motion[2, 1, 0:1, :]
    spread_left, spread_last = upsampled([row_left, own_last])
    for t in range(TILES):
        wet = floor_tile(1, t, True)
        coef[0, t] = narrowed(wet)
        coef[1, t] = narrowed(wet * roll(wet, -1, 0))
        coef[7, t] = floor_tile(0, t, wide)
    for t in range(TILES):
        wet = coef[0, t]
        coef[8, t] = wet * east(lambda i: coef[0, i], t)
    for t in range(TILES):
        for at, depth_side in ((1, 0), (8, 1)):
            face = coef[at, t]
            near = [roll(face, -1, 0), roll(face, 1, 0)]
            tile = functools.partial(lambda at, i: coef[at, i], at)
            near += [east(tile, t), west(tile, t)]
            total = near[0] + near[1] + near[2] + near[3]
            for j in range(4):
                coef[at + 1 + j, t] = VISCOSITY * face * near[j]
            coef[at + 5, t] = face - VISCOSITY * face * total
        depth = coef[7, t]
        coef[14, t] = depth + east(lambda i: coef[7, i], t)
    for t in range(TILES):
        depth = coef[7, t]
        coef[7, t] = depth + roll(depth, -1, 0)
        coef[1, t] = WAVE_STEP * 0.5 * coef[1, t]
        coef[8, t] = WAVE_STEP * 0.5 * coef[8, t]
        for f in range(3):
            at = (f * TILES + t) * 8
            near, top = inbox.right(ocean_at + at), inbox.left(ocean_at + at)
            first, second = ocean[f, t, 0:8, :], ocean[f, t, 8:16, :]
            wet = coef[0, t]
            if f == 0:
                first = first + UPLIFT_GAIN * wet[0:8] * spread_left[t : t + 1]
                near = near + UPLIFT_GAIN * wet[16:24] * spread_last[t : t + 1]
            if wide:
                far = inbox.right(more_at + at)
                value = jnp.concatenate([first, second, near, joined(far, top)], axis=0)
            else:
                value = jnp.concatenate([first, second, joined(near, top)], axis=0)
            if f == 0:
                height[t] = value
            else:
                flow[0, f - 1, t] = value
        coef[0, t] = WAVE_STEP * coef[0, t]
    for step in range(NSUB):
        old, new = step % 2, (step + 1) % 2
        for t in range(TILES):
            m, n = flow[old, 0, t], flow[old, 1, t]
            spill = (m - roll(m, 1, 0)) + (n - west(lambda i: flow[old, 1, i], t))
            height[t] = height[t] - coef[0, t] * spill
        for t in range(TILES):
            h = height[t]
            ahead = [roll(h, -1, 0), east(lambda i: height[i], t)]
            for d in range(2):
                at = 1 + 7 * d
                tile = functools.partial(lambda d, i: flow[old, d, i], d)
                q = flow[old, d, t]
                slope = (coef[at + 6, t] + h + ahead[d]) * (ahead[d] - h)
                value = coef[at + 5, t] * q - coef[at, t] * slope
                value = value + coef[at + 1, t] * roll(q, -1, 0)
                value = value + coef[at + 2, t] * roll(q, 1, 0)
                value = value + coef[at + 3, t] * east(tile, t)
                value = value + coef[at + 4, t] * west(tile, t)
                flow[new, d, t] = value


def step_kernel(kind, last, is_first, *refs):
    parity, base_one, base_two = refs[0:3]
    refs = refs[3:]
    if is_first:
        one, two = base_one, base_two
    else:
        one, two = refs[0:2]
        refs = refs[2:]
    motion, stress, solid, ocean, floor = refs[0:5]
    if last:
        motion_out, stress_out, surface_out, momentum_out = refs[5:9]
        refs = refs[9:]
    else:
        motion_out, stress_out, ocean_out, send_one, send_two = refs[5:10]
        refs = refs[10:]
    coef, height, flow, edge, speed = refs
    slabs = motion.shape[2] // 8
    part, ocean_at, extra_at, more_at, static_at = offsets(slabs)
    even = parity[0] == 0
    base = Receiver(even, base_one, base_two)
    inbox = Receiver(even, one, two)

    def extra_row(take):
        return jnp.concatenate([take(extra_at)[0:1], take(extra_at + 8)[0:1]], axis=1)

    row_left = extra_row(inbox.left)
    loaded = None if is_first else -LOAD_GAIN * extra_row(inbox.right)
    ocean_part(inbox, base, slabs, motion, ocean, floor, kind, coef, height, flow, row_left)
    blocks = 3 if last else 2
    sums = [[] for _ in range(blocks)]
    for t in range(TILES):
        h = height[t]
        wet = (1.0 / WAVE_STEP) * coef[0, t]
        for b in range(blocks):
            rows = slice(8 * b, 8 * b + 8)
            sums[b].append(jnp.sum(wet[rows] * h[rows], axis=0, keepdims=True))
        if last:
            if t < TILES - 1:
                lanes = slice(LANES * t, LANES * t + LANES)
                surface_out[:, lanes] = h[0:16]
                for d in range(2):
                    momentum_out[d, :, lanes] = flow[NSUB % 2, d, t, 0:16, :]
        else:
            ocean_out[0, t] = h[0:16]
            for d in range(2):
                ocean_out[1 + d, t] = flow[NSUB % 2, d, t, 0:16, :]
    means = block_means(sums)

    def old(f, row):
        def get(k):
            value = stress[f, row, 8 * k : 8 * k + 8, :]
            if (f, row, k) == (2, 1, 0) and loaded is not None:
                value = jnp.where(iota(value.shape, 0) == 0, loaded, value)
            return value

        return get

    def new(f, row):
        return lambda k: speed[f, row, 8 * k : 8 * k + 8, :]

    for k in range(slabs):
        z = slice(8 * k, 8 * k + 8)
        xx = [stress[0, 0, z, :], stress[0, 1, z, :], inbox.solid(1, 2 * part, k, slabs)]
        xy = [inbox.solid(-1, part, k, slabs), stress[3, 0, z, :], stress[3, 1, z, :]]
        xz = [inbox.solid(-1, 2 * part, k, slabs), stress[4, 0, z, :], stress[4, 1, z, :]]
        rate_left = SOLID_STEP * base.solid(-1, more_at, k, slabs)
        rate_right = SOLID_STEP * base.solid(1, more_at, k, slabs)
        speed[0, 2, z, :] = inbox.solid(-1, 0, k, slabs) + rate_left * xx[0]
        speed[1, 2, z, :] = inbox.solid(1, 0, k, slabs) - rate_right * xy[2]
        speed[2, 2, z, :] = inbox.solid(1, part, k, slabs) - rate_right * xz[2]
        for row in range(2):
            rate = SOLID_STEP * solid[0, row, z, :]
            yy, zz, yz = stress[1, row, z, :], old(2, row)(k), stress[5, row, z, :]
            mid_xy, mid_xz = xy[row + 1], xz[row + 1]
            force_x = (xx[row + 1] - xx[row]) + (mid_xy - prev_lane(mid_xy))
            force_x = force_x + (mid_xz - below(old(4, row), k))
            force_y = (mid_xy - xy[row]) + (next_lane(yy) - yy) + (yz - below(old(5, row), k))
            force_z = (mid_xz - xz[row]) + (yz - prev_lane(yz))
            force_z = force_z + (above(old(2, row), k, slabs) - zz)
            for f, force in enumerate((force_x, force_y, force_z)):
                value = motion[f, row, z, :] + rate * force
                speed[f, row, z, :] = value
                if last:
                    motion_out[f, row, z, :] = value[:, :LANES]
                else:
                    motion_out[f, row, z, :] = value
    width = LANES if last else 2 * LANES
    for k in range(slabs):
        z = slice(8 * k, 8 * k + 8)
        x_of = [speed[0, 2, z, :], speed[0, 0, z, :], speed[0, 1, z, :]]
        y_of = [speed[1, 0, z, :], speed[1, 1, z, :], speed[1, 2, z, :]]
        z_of = [speed[2, 0, z, :], speed[2, 1, z, :], speed[2, 2, z, :]]
        for row in range(2):
            vx, vy, vz = x_of[row + 1], y_of[row], z_of[row]
            strain_x = vx - x_of[row]
            strain_y = vy - prev_lane(vy)
            strain_z = vz - below(new(2, row), k)
            shear = SOLID_STEP * solid[2, row, z, :]
            lame = SOLID_STEP * solid[1, row, z, :]
            common = lame * (strain_x + strain_y + strain_z)
            twice = shear + shear
            rates = [common + twice * strain for strain in (strain_x, strain_y, strain_z)]
            rates.append(shear * ((next_lane(vx) - vx) + (y_of[row + 1] - vy)))
            rates.append(shear * ((above(new(0, row), k, slabs) - vx) + (z_of[row + 1] - vz)))
            rates.append(shear * ((above(new(1, row), k, slabs) - vy) + (next_lane(vz) - vz)))
            for f in range(6):
                value = stress[f, row, z, :] + rates[f]
                stress_out[f, row, z, :] = value[:, :width]
    stress_out[2, 0, 0:1, :] = -LOAD_GAIN * means[1][:, :width]
    if last:
        stress_out[2, 1, 0:1, :] = -LOAD_GAIN * means[2][:, :width]
        return
    out = Sender(even, send_one, send_two)
    next_kind = "last" if edge else "usual"
    finish(
        out, slabs, motion_out, stress_out, solid, ocean_out, floor.at[1], means[0], next_kind
    )


def swap(size, start):
    pairs = []
    for i in range(start, size - 1, 2):
        pairs += [(i, i + 1), (i + 1, i)]
    return pairs


def exchanged(first, second, axis):
    size = lax.axis_size(axis)
    return (
        lax.ppermute(first, axis, swap(size, 0)),
        lax.ppermute(second, axis, swap(size, 1)),
    )


def body(motion, stress, buoyancy, lame_first, lame_shear, surface, momentum, bathymetry, wet_mask):
    depth_cells = motion.shape[2]
    slabs = depth_cells // 8
    f32 = jnp.float32

    def array(*shape):
        return jax.ShapeDtypeStruct(shape, f32)

    def call(kernel, outs, args, scratch=()):
        specs = [pl.BlockSpec(memory_space=pltpu.SMEM)]
        specs += [pl.BlockSpec(memory_space=pltpu.VMEM)] * (len(args) - 1)
        return pl.pallas_call(
            kernel,
            out_shape=outs,
            in_specs=specs,
            out_specs=tuple(pl.BlockSpec(memory_space=pltpu.VMEM) for _ in outs),
            scratch_shapes=list(scratch),
            interpret=INTERPRET,
        )(*args)

    parity = jnp.stack([lax.axis_index("gx") % 2, lax.axis_index("gy") % 2]).astype(jnp.int32)
    own = (
        motion, stress, buoyancy, lame_first, lame_shear, surface, momentum, bathymetry, wet_mask,
    )
    rows = pack_y_rows(slabs)
    send = call(pack_y_kernel, (array(rows, LANES),) * 2, (parity, *own))
    received = exchanged(*send, "gy")
    state = (
        array(3, 2, depth_cells, 256),
        array(6, 2, depth_cells, 256),
    )
    rows = payload_rows(slabs, "first")
    outs = (
        *state,
        array(3, 2, depth_cells, 256),
        array(3, TILES, 16, LANES),
        array(2, TILES, 16, LANES),
        array(rows, LANES),
        array(rows, LANES),
    )
    motion, stress, solid, ocean, floor, *send = call(start_kernel, outs, (parity, *own, *received))
    base = None
    for step in range(STEPS):
        received = exchanged(*send, "gx")
        last = step == STEPS - 1
        if step == 0:
            base = received
            inputs = (parity, *base)
        else:
            inputs = (parity, *base, *received)
        inputs = (*inputs, motion, stress, solid, ocean, floor)
        height = 32 if last else 24
        scratch = (
            pltpu.VMEM((15, TILES, height, LANES), f32),
            pltpu.VMEM((TILES, height, LANES), f32),
            pltpu.VMEM((2, 2, TILES, height, LANES), f32),
            pltpu.VMEM((3, 3, depth_cells, 256), f32),
        )
        if last:
            outs = (
                array(3, 2, depth_cells, LANES),
                array(6, 2, depth_cells, LANES),
                array(16, 8 * LANES),
                array(2, 16, 8 * LANES),
            )
        else:
            rows = payload_rows(slabs, "last" if step == STEPS - 2 else "usual")
            outs = (*state, array(3, TILES, 16, LANES), array(rows, LANES), array(rows, LANES))
        kernel = functools.partial(
            run_step, "last" if last else "usual", last, step == 0, step == STEPS - 2
        )
        results = call(kernel, outs, inputs, scratch)
        if not last:
            motion, stress, ocean, *send = results
    return results


def run_step(kind, last, is_first, edge, *refs):
    coef, height, flow, speed = refs[-4:]
    step_kernel(kind, last, is_first, *refs[:-4], coef, height, flow, edge, speed)


def solution(mesh):
    return jax.shard_map(
        body,
        mesh=mesh,
        in_specs=(
            P(None, "gx", None, "gy"),
            P(None, "gx", None, "gy"),
            P("gx", None, "gy"),
            P("gx", None, "gy"),
            P("gx", None, "gy"),
            P("gx", "gy"),
            P(None, "gx", "gy"),
            P("gx", "gy"),
            P("gx", "gy"),
        ),
        out_specs=(
            P(None, "gx", None, "gy"),
            P(None, "gx", None, "gy"),
            P("gx", "gy"),
            P(None, "gx", "gy"),
        ),
        check_vma=False,
    )
```

```python
import functools

import jax
import jax.numpy as jnp
from jax import lax
from jax.experimental import pallas as pl
from jax.experimental.pallas import tpu as pltpu
from jax.sharding import PartitionSpec as P

STEPS = 4
NSUB = 4
SOLID_STEP = 0.2
WAVE_STEP = 0.1
VISCOSITY = 0.05
UPLIFT_GAIN = 0.25
LOAD_GAIN = 8.0

INTERPRET = False
VMEM_LIMIT = 20 << 20
LANES = 128
TILES = 9
UNITS = 3 * TILES
FLOOR_UNITS = 2 * TILES


def iota(shape, dim):
    return lax.broadcasted_iota(jnp.int32, shape, dim)


def roll(value, shift, axis):
    shift = shift % value.shape[axis]
    return value if shift == 0 else pltpu.roll(value, shift, axis)


def prev_lane(value):
    return roll(value, 1, 1)


def next_lane(value):
    return roll(value, -1, 1)


def below(get, k):
    current = roll(get(k), 1, 0)
    other = roll(get(k - 1), 1, 0) if k > 0 else jnp.zeros_like(current)
    return jnp.where(iota(current.shape, 0) == 0, other, current)


def above(get, k, slabs):
    current = roll(get(k), -1, 0)
    other = roll(get(k + 1), -1, 0) if k < slabs - 1 else jnp.zeros_like(current)
    return jnp.where(iota(current.shape, 0) == 7, other, current)


def expander():
    shape = (LANES, LANES)
    return jnp.where(iota(shape, 0) == iota(shape, 1) >> 3, 1.0, 0.0)


def reducer():
    shape = (LANES, LANES)
    return jnp.where(iota(shape, 0) >> 3 == iota(shape, 1), 1.0 / 64.0, 0.0)


def exact_dot(left, right):
    return jnp.dot(
        left, right, precision=lax.Precision.HIGHEST, preferred_element_type=jnp.float32
    )


def upsampled(rows):
    lane, line = iota((8, LANES), 1), iota((8, LANES), 0)
    stack = []
    for row in rows:
        own = jnp.broadcast_to(row[:, :LANES], (8, LANES))
        halo = jnp.broadcast_to(row[:, LANES:], (8, LANES))
        tiles = own
        for t in range(1, 8):
            tiles = jnp.where(line == t, roll(own, -16 * t, 1), tiles)
        stack += [tiles, jnp.where(lane < 4, halo, roll(halo, 16, 1))]
    spread = exact_dot(jnp.concatenate(stack, axis=0), expander())
    return [spread[16 * i : 16 * i + 16] for i in range(len(rows))]


def block_means(sums):
    lane, line = iota((8, LANES), 1), iota((8, LANES), 0)
    stack = []
    for tiles in sums:
        wide = [jnp.broadcast_to(tile, (8, LANES)) for tile in tiles]
        own = wide[0]
        for t in range(1, 8):
            own = jnp.where(line == t, wide[t], own)
        stack += [own, wide[8]]
    mean = exact_dot(jnp.concatenate(stack, axis=0), reducer())
    rows = []
    for i in range(len(sums)):
        tiles, last = mean[16 * i : 16 * i + 8], mean[16 * i + 8 : 16 * i + 16]
        own = jnp.zeros((8, LANES), jnp.float32)
        for t in range(8):
            own = jnp.where((line == t) & (lane >> 4 == t), roll(tiles, 16 * t, 1), own)
        own = jnp.sum(own, axis=0, keepdims=True)
        halo = jnp.where(lane < 4, last, jnp.where(lane >= 124, roll(last, 112, 1), 0.0))
        rows.append(jnp.concatenate([own, halo[0:1]], axis=1))
    return rows


class Sender:
    def __init__(self, even, first_ref, second_ref):
        self.even, self.first, self.second = even, first_ref, second_ref

    def put(self, at, right, left):
        end = at + right.shape[0]
        self.first[at:end, :] = jnp.where(self.even, right, left)
        self.second[at:end, :] = jnp.where(self.even, left, right)

    def put_solid(self, at, slabs, right, left):
        lane = iota((8, LANES), 1)
        tails = [jnp.zeros((8, LANES), jnp.float32) for _ in range(2)]
        for k in range(slabs):
            here = (lane >= 8 * k) & (lane < 8 * k + 8)
            values = (right(k), left(k))
            for i, value in enumerate(values):
                tails[i] = jnp.where(here, roll(value[:, LANES:], 4 + 8 * k, 1), tails[i])
            self.put(at + 8 * k, values[0][:, :LANES], values[1][:, :LANES])
        self.put(at + 8 * slabs, *tails)


    def put_halves(self, at, units):
        low = iota((8, LANES), 0) < 4
        for i in range(0, len(units), 2):
            (lower, upper), (lower2, upper2) = units[i], units[min(i + 1, len(units) - 1)]
            right = jnp.where(low, roll(upper, 4, 0), upper2)
            left = jnp.where(low, lower, roll(lower2, 4, 0))
            self.put(at + 4 * i, right, left)


class Receiver:
    def __init__(self, even, first_ref, second_ref):
        self.even, self.first, self.second = even, first_ref, second_ref

    def right(self, at):
        return jnp.where(self.even, self.first[at : at + 8, :], self.second[at : at + 8, :])

    def left(self, at):
        return jnp.where(self.even, self.second[at : at + 8, :], self.first[at : at + 8, :])

    def halves(self, at, unit):
        at = at + 8 * (unit // 2)
        near, top = self.right(at), self.left(at)
        near = roll(near, 4, 0) if unit % 2 else near
        top = top if unit % 2 else roll(top, 4, 0)
        return near, top

    def solid(self, side, at, k, slabs):
        take = self.right if side > 0 else self.left
        tail = roll(take(at + 8 * slabs), -(4 + 8 * k), 1)
        return jnp.concatenate([take(at + 8 * k), tail], axis=1)


def offsets(slabs):
    part = 8 * slabs + 8
    ocean = 3 * part
    extra = ocean + 8 * ((UNITS + 1) // 2)
    more = extra + 16
    return part, ocean, extra, more


def payload_rows(slabs, kind):
    part, _, _, more = offsets(slabs)
    return {
        "first": more + part + 8 * ((FLOOR_UNITS + TILES + 1) // 2),
        "usual": more,
        "last": more + 8 * (UNITS + FLOOR_UNITS),
    }[kind]


def finish(out, slabs, motion, stress, buoyancy, ocean, floor, mean_row, kind):
    part, ocean_at, extra_at, more_at = offsets(slabs)
    low = iota((8, LANES), 0) < 4

    def get(ref, field, row):
        return lambda k: ref[field, row, 8 * k : 8 * k + 8, :]

    def rate(row, k):
        return SOLID_STEP * buoyancy[0, row, 8 * k : 8 * k + 8, :]

    def sum_x(k):
        xx, xy, xz = (get(stress, f, 1) for f in (0, 3, 4))
        mid = xy(k)
        force = (mid - prev_lane(mid)) + (xz(k) - below(xz, k)) - xx(k)
        return get(motion, 0, 1)(k) + rate(1, k) * force

    def sum_y(k):
        xy, yy, yz = (get(stress, f, 0) for f in (3, 1, 5))
        mid = yy(k)
        force = xy(k) + (next_lane(mid) - mid) + (yz(k) - below(yz, k))
        return get(motion, 1, 0)(k) + rate(0, k) * force

    def sum_z(k):
        xz, yz, zz = (get(stress, f, 0) for f in (4, 5, 2))
        mid = yz(k)
        force = xz(k) + (mid - prev_lane(mid)) + (above(zz, k, slabs) - zz(k))
        return get(motion, 2, 0)(k) + rate(0, k) * force

    out.put_solid(0, slabs, sum_x, sum_y)
    out.put_solid(part, slabs, get(stress, 3, 1), sum_z)
    out.put_solid(2 * part, slabs, get(stress, 4, 1), get(stress, 0, 0))
    (spread,) = upsampled([motion[2, 0, 0:1, :]])
    for t in range(TILES):
        ocean[0, t, 8:16, :] = (
            ocean[0, t, 8:16, :] + UPLIFT_GAIN * floor[1, t, 8:16, :] * spread[t : t + 1]
        )

    def units(ref, fields):
        pairs = [(f, t) for f in range(fields) for t in range(TILES)]
        return [(ref[f, t, 0:8, :], ref[f, t, 8:16, :]) for f, t in pairs]

    out.put_halves(ocean_at, units(ocean, 3))
    top = motion[2, 1, 0:8, :]
    mean_row = jnp.zeros((8, 256), jnp.float32) if mean_row is None else mean_row
    mean_row = jnp.broadcast_to(mean_row, (8, 256))
    for i in range(2):
        lanes = slice(LANES * i, LANES * i + LANES)
        out.put(extra_at + 8 * i, top[:, lanes], mean_row[:, lanes])
    if kind == "first":
        out.put_solid(more_at, slabs, get(buoyancy, 0, 1), get(buoyancy, 0, 0))
        faces = []
        for t in range(TILES):
            wet = floor[1, t, :, :]
            faces.append(((wet * roll(wet, -1, 0))[0:8], wet[8:16]))
        out.put_halves(more_at + part, units(floor, 2) + faces)
    if kind == "last":
        for i, (lower, upper) in enumerate(units(ocean, 3) + units(floor, 2)):
            value = jnp.where(low, upper, lower)
            out.put(more_at + 8 * i, value, value)


def pack_y_kernel(
    parity, motion, stress, buoyancy, first, shear, surface, momentum, depth, wet, one, two
):
    even = parity[1] == 0
    out = Sender(even, one, two)
    slabs = motion.shape[2] // 8
    lane = iota((8, LANES), 1)
    fields = [(motion, f) for f in range(3)] + [(stress, f) for f in range(6)]
    fields += [(buoyancy, None), (first, None), (shear, None)]
    count, at = 0, 0
    right = left = jnp.zeros((8, LANES), jnp.float32)
    for ref, f in fields:
        for row in range(2):
            for k in range(slabs):
                z = slice(8 * k, 8 * k + 8)
                value = ref[row, z, :] if f is None else ref[f, row, z, :]
                here = lane >> 2 == count
                right = jnp.where(here, roll(value, 4 * count + 4, 1), right)
                left = jnp.where(here, roll(value, 4 * count, 1), left)
                count += 1
                if count == 32:
                    out.put(at, right, left)
                    count, at = 0, at + 8
    if count:
        out.put(at, right, left)
        count, at = 0, at + 8
    width = surface.shape[1]
    for ref, f in ((surface, None), (momentum, 0), (momentum, 1), (depth, None), (wet, None)):
        for group in range(2):
            rows = slice(8 * group, 8 * group + 8)
            ends = []
            for lanes in (slice(0, LANES), slice(width - LANES, width)):
                value = ref[rows, lanes] if f is None else ref[f, rows, lanes]
                ends.append(value.astype(jnp.float32))
            here = lane >> 5 == count
            right = jnp.where(here, roll(ends[1], 32 * count + 32, 1), right)
            left = jnp.where(here, roll(ends[0], 32 * count, 1), left)
            count += 1
            if count == 4:
                out.put(at, right, left)
                count, at = 0, at + 8
    if count:
        out.put(at, right, left)


def pack_y_rows(slabs):
    return 8 * (-(-24 * slabs // 32) + 3)


def start_kernel(
    parity, motion, stress, buoyancy, first, shear, surface, momentum, depth, wet, one, two,
    motion_out, stress_out, solid_out, ocean_out, floor_out, send_one, send_two,
):
    inbox = Receiver(parity[1] == 0, one, two)
    slabs = motion.shape[2] // 8
    lane = iota((8, LANES), 1)
    fields = [(motion, f, motion_out, f) for f in range(3)]
    fields += [(stress, f, stress_out, f) for f in range(6)]
    fields += [(ref, None, solid_out, f) for f, ref in enumerate((buoyancy, first, shear))]
    count, at = 0, 0
    for ref, f, target, g in fields:
        for row in range(2):
            for k in range(slabs):
                z = slice(8 * k, 8 * k + 8)
                value = ref[row, z, :] if f is None else ref[f, row, z, :]
                if count == 0:
                    packed = inbox.right(at), inbox.left(at)
                after = roll(packed[0], -4 * count, 1)
                before = roll(packed[1], 124 - 4 * count, 1)
                halo = jnp.where(lane < 4, after, jnp.where(lane >= 124, before, 0.0))
                target[g, row, z, 0:LANES] = value
                target[g, row, z, LANES : 2 * LANES] = halo
                count += 1
                if count == 32:
                    count, at = 0, at + 8
    if count:
        count, at = 0, at + 8
    targets = ((surface, None), (momentum, 0), (momentum, 1), (depth, None), (wet, None))
    for i, (ref, f) in enumerate(targets):
        for group in range(2):
            rows = slice(8 * group, 8 * group + 8)
            if count == 0:
                packed = inbox.right(at), inbox.left(at)
            after = roll(packed[0], -32 * count, 1)
            before = roll(packed[1], 96 - 32 * count, 1)
            halo = jnp.where(lane < 32, after, jnp.where(lane >= 96, before, 0.0))
            for t in range(TILES):
                if t == TILES - 1:
                    value = halo
                else:
                    lanes = slice(LANES * t, LANES * t + LANES)
                    value = ref[rows, lanes] if f is None else ref[f, rows, lanes]
                    value = value.astype(jnp.float32)
                if i < 3:
                    ocean_out[i, t, rows, :] = value
                else:
                    floor_out[i - 3, t, rows, :] = value
            count += 1
            if count == 4:
                count, at = 0, at + 8
    out = Sender(parity[0] == 0, send_one, send_two)
    finish(out, slabs, motion_out, stress_out, solid_out, ocean_out, floor_out, None, "first")


def coefficients(floor_tile, after, coef, east, west):
    for t in range(TILES):
        wet = floor_tile(1, t)
        coef[0, t] = wet
        face = wet * roll(wet, -1, 0)
        if after is not None:
            low = iota((8, LANES), 0) < 4
            face = jnp.concatenate([face[0:16], jnp.where(low, after(t), face[16:24])], axis=0)
        coef[1, t] = face
        coef[7, t] = floor_tile(0, t)
    for t in range(TILES):
        coef[8, t] = coef[0, t] * east(lambda i: coef[0, i], t)
    for t in range(TILES):
        for at in (1, 8):
            face = coef[at, t]
            near = [roll(face, -1, 0), roll(face, 1, 0)]
            tile = functools.partial(lambda at, i: coef[at, i], at)
            near += [east(tile, t), west(tile, t)]
            total = near[0] + near[1] + near[2] + near[3]
            for j in range(4):
                coef[at + 1 + j, t] = VISCOSITY * face * near[j]
            coef[at + 5, t] = face - VISCOSITY * face * total
        coef[14, t] = coef[7, t] + east(lambda i: coef[7, i], t)
    for t in range(TILES):
        depth = coef[7, t]
        coef[7, t] = depth + roll(depth, -1, 0)
        coef[1, t] = WAVE_STEP * 0.5 * coef[1, t]
        coef[8, t] = WAVE_STEP * 0.5 * coef[8, t]


def ocean_part(
    inbox, base, slabs, motion, ocean, floor, wide, ready, coef, height, flow, row_left
):
    part, ocean_at, _, more_at = offsets(slabs)
    low = iota((8, LANES), 0) < 4

    def joined(upper, lower):
        return jnp.where(low, upper, lower)

    def floor_tile(f, t):
        near, top = base.halves(more_at + part, f * TILES + t)
        own = floor[f, t, :, :]
        if wide:
            far = inbox.right(more_at + 8 * (UNITS + f * TILES + t))
            return jnp.concatenate([own, joined(near, far), joined(far, top)], axis=0)
        return jnp.concatenate([own, joined(near, top)], axis=0)

    lane0 = lambda rows: iota((rows, LANES), 1) == 0
    lane127 = lambda rows: iota((rows, LANES), 1) == LANES - 1

    def west(tile, t):
        mine, other = roll(tile(t), 1, 1), roll(tile((t - 1) % TILES), 1, 1)
        return jnp.where(lane0(mine.shape[0]), other, mine)

    def east(tile, t):
        mine, other = roll(tile(t), -1, 1), roll(tile((t + 1) % TILES), -1, 1)
        return jnp.where(lane127(mine.shape[0]), other, mine)

    if not ready:
        after = lambda t: base.halves(more_at + part, 2 * TILES + t)[0]
        coefficients(floor_tile, None if wide else after, coef, east, west)
    own_last = motion[2, 1, 0:1, :]
    spread_left, spread_last = upsampled([row_left, own_last])
    for t in range(TILES):
        wet = coef[0, t]
        for f in range(3):
            near, top = inbox.halves(ocean_at, f * TILES + t)
            first, second = ocean[f, t, 0:8, :], ocean[f, t, 8:16, :]
            if wide:
                far = inbox.right(more_at + 8 * (f * TILES + t))
                near = joined(near, far)
            if f == 0:
                first = first + UPLIFT_GAIN * wet[0:8] * spread_left[t : t + 1]
                near = near + UPLIFT_GAIN * wet[16:24] * spread_last[t : t + 1]
            if wide:
                value = jnp.concatenate([first, second, near, joined(far, top)], axis=0)
            else:
                value = jnp.concatenate([first, second, joined(near, top)], axis=0)
            if f == 0:
                height[t] = value
            else:
                flow[0, f - 1, t] = value
    for step in range(NSUB):
        old, new = step % 2, (step + 1) % 2
        for t in range(TILES):
            m, n = flow[old, 0, t], flow[old, 1, t]
            spill = (m - roll(m, 1, 0)) + (n - west(lambda i: flow[old, 1, i], t))
            height[t] = height[t] - coef[0, t] * (WAVE_STEP * spill)
        for t in range(TILES):
            h = height[t]
            ahead = [roll(h, -1, 0), east(lambda i: height[i], t)]
            for d in range(2):
                at = 1 + 7 * d
                tile = functools.partial(lambda d, i: flow[old, d, i], d)
                q = flow[old, d, t]
                slope = (coef[at + 6, t] + h + ahead[d]) * (ahead[d] - h)
                value = coef[at + 5, t] * q - coef[at, t] * slope
                value = value + coef[at + 1, t] * roll(q, -1, 0)
                value = value + coef[at + 2, t] * roll(q, 1, 0)
                value = value + coef[at + 3, t] * east(tile, t)
                value = value + coef[at + 4, t] * west(tile, t)
                flow[new, d, t] = value


def step_kernel(last, is_first, edge, *refs):
    parity, refs = refs[0], list(refs[1:])

    def take(count):
        taken = refs[:count]
        del refs[:count]
        return taken

    base_one, base_two = take(2)
    one, two = (base_one, base_two) if is_first else take(2)
    motion, stress, solid, ocean, floor = take(5)
    ready = not (is_first or last)
    if ready:
        (coef,) = take(1)
    if last:
        motion_out, stress_out, surface_out, momentum_out = take(4)
    else:
        motion_out, stress_out, ocean_out, send_one, send_two = take(5)
    if not ready:
        (coef,) = take(1)
    height, flow, speed = take(3)
    slabs = motion.shape[2] // 8
    part, _, extra_at, more_at = offsets(slabs)
    even = parity[0] == 0
    base = Receiver(even, base_one, base_two)
    inbox = Receiver(even, one, two)

    def extra_row(take):
        return jnp.concatenate([take(extra_at)[0:1], take(extra_at + 8)[0:1]], axis=1)

    row_left = extra_row(inbox.left)
    loaded = None if is_first else -LOAD_GAIN * extra_row(inbox.right)
    ocean_part(
        inbox, base, slabs, motion, ocean, floor, last, ready, coef, height, flow, row_left
    )
    blocks = 3 if last else 2
    sums = [[] for _ in range(blocks)]
    for t in range(TILES):
        h = height[t]
        wet = coef[0, t]
        for b in range(blocks):
            rows = slice(8 * b, 8 * b + 8)
            sums[b].append(jnp.sum(wet[rows] * h[rows], axis=0, keepdims=True))
        if last:
            if t < TILES - 1:
                lanes = slice(LANES * t, LANES * t + LANES)
                surface_out[:, lanes] = h[0:16]
                for d in range(2):
                    momentum_out[d, :, lanes] = flow[NSUB % 2, d, t, 0:16, :]
        else:
            ocean_out[0, t] = h[0:16]
            for d in range(2):
                ocean_out[1 + d, t] = flow[NSUB % 2, d, t, 0:16, :]
    means = block_means(sums)

    def old(f, row):
        def get(k):
            value = stress[f, row, 8 * k : 8 * k + 8, :]
            if (f, row, k) == (2, 1, 0) and loaded is not None:
                value = jnp.where(iota(value.shape, 0) == 0, loaded, value)
            return value

        return get

    def new(f, row):
        return lambda k: speed[f, row, 8 * k : 8 * k + 8, :]

    for k in range(slabs):
        z = slice(8 * k, 8 * k + 8)
        xx = [stress[0, 0, z, :], stress[0, 1, z, :], inbox.solid(1, 2 * part, k, slabs)]
        xy = [inbox.solid(-1, part, k, slabs), stress[3, 0, z, :], stress[3, 1, z, :]]
        xz = [inbox.solid(-1, 2 * part, k, slabs), stress[4, 0, z, :], stress[4, 1, z, :]]
        rate_left = SOLID_STEP * base.solid(-1, more_at, k, slabs)
        rate_right = SOLID_STEP * base.solid(1, more_at, k, slabs)
        speed[0, 2, z, :] = inbox.solid(-1, 0, k, slabs) + rate_left * xx[0]
        speed[1, 2, z, :] = inbox.solid(1, 0, k, slabs) - rate_right * xy[2]
        speed[2, 2, z, :] = inbox.solid(1, part, k, slabs) - rate_right * xz[2]
        for row in range(2):
            rate = SOLID_STEP * solid[0, row, z, :]
            yy, zz, yz = stress[1, row, z, :], old(2, row)(k), stress[5, row, z, :]
            mid_xy, mid_xz = xy[row + 1], xz[row + 1]
            force_x = (xx[row + 1] - xx[row]) + (mid_xy - prev_lane(mid_xy))
            force_x = force_x + (mid_xz - below(old(4, row), k))
            force_y = (mid_xy - xy[row]) + (next_lane(yy) - yy) + (yz - below(old(5, row), k))
            force_z = (mid_xz - xz[row]) + (yz - prev_lane(yz))
            force_z = force_z + (above(old(2, row), k, slabs) - zz)
            for f, force in enumerate((force_x, force_y, force_z)):
                value = motion[f, row, z, :] + rate * force
                speed[f, row, z, :] = value
                if last:
                    motion_out[f, row, z, :] = value[:, :LANES]
                else:
                    motion_out[f, row, z, :] = value
    width = LANES if last else 2 * LANES
    for k in range(slabs):
        z = slice(8 * k, 8 * k + 8)
        x_of = [speed[0, 2, z, :], speed[0, 0, z, :], speed[0, 1, z, :]]
        y_of = [speed[1, 0, z, :], speed[1, 1, z, :], speed[1, 2, z, :]]
        z_of = [speed[2, 0, z, :], speed[2, 1, z, :], speed[2, 2, z, :]]
        for row in range(2):
            vx, vy, vz = x_of[row + 1], y_of[row], z_of[row]
            strain_x = vx - x_of[row]
            strain_y = vy - prev_lane(vy)
            strain_z = vz - below(new(2, row), k)
            shear = SOLID_STEP * solid[2, row, z, :]
            lame = SOLID_STEP * solid[1, row, z, :]
            common = lame * (strain_x + strain_y + strain_z)
            twice = shear + shear
            rates = [common + twice * strain for strain in (strain_x, strain_y, strain_z)]
            rates.append(shear * ((next_lane(vx) - vx) + (y_of[row + 1] - vy)))
            rates.append(shear * ((above(new(0, row), k, slabs) - vx) + (z_of[row + 1] - vz)))
            rates.append(shear * ((above(new(1, row), k, slabs) - vy) + (next_lane(vz) - vz)))
            for f in range(6):
                value = stress[f, row, z, :] + rates[f]
                stress_out[f, row, z, :] = value[:, :width]
    stress_out[2, 0, 0:1, :] = -LOAD_GAIN * means[1][:, :width]
    if last:
        stress_out[2, 1, 0:1, :] = -LOAD_GAIN * means[2][:, :width]
        return
    out = Sender(even, send_one, send_two)
    next_kind = "last" if edge else "usual"
    finish(out, slabs, motion_out, stress_out, solid, ocean_out, floor, means[0], next_kind)


def swap(size, start):
    pairs = []
    for i in range(start, size - 1, 2):
        pairs += [(i, i + 1), (i + 1, i)]
    return pairs


def exchanged(first, second, axis):
    size = lax.axis_size(axis)
    return (
        lax.ppermute(first, axis, swap(size, 0)),
        lax.ppermute(second, axis, swap(size, 1)),
    )


def body(motion, stress, buoyancy, lame_first, lame_shear, surface, momentum, bathymetry, wet_mask):
    depth_cells = motion.shape[2]
    slabs = depth_cells // 8
    f32 = jnp.float32

    def array(*shape):
        return jax.ShapeDtypeStruct(shape, f32)

    def call(kernel, outs, args, scratch=()):
        specs = [pl.BlockSpec(memory_space=pltpu.SMEM)]
        specs += [pl.BlockSpec(memory_space=pltpu.VMEM)] * (len(args) - 1)
        return pl.pallas_call(
            kernel,
            out_shape=outs,
            in_specs=specs,
            out_specs=tuple(pl.BlockSpec(memory_space=pltpu.VMEM) for _ in outs),
            scratch_shapes=list(scratch),
            compiler_params=pltpu.CompilerParams(vmem_limit_bytes=VMEM_LIMIT),
            interpret=INTERPRET,
        )(*args)

    parity = jnp.stack([lax.axis_index("gx") % 2, lax.axis_index("gy") % 2]).astype(jnp.int32)
    own = (
        motion, stress, buoyancy, lame_first, lame_shear, surface, momentum, bathymetry, wet_mask,
    )
    rows = pack_y_rows(slabs)
    send = call(pack_y_kernel, (array(rows, LANES),) * 2, (parity, *own))
    received = exchanged(*send, "gy")
    state = (
        array(3, 2, depth_cells, 256),
        array(6, 2, depth_cells, 256),
    )
    rows = payload_rows(slabs, "first")
    outs = (
        *state,
        array(3, 2, depth_cells, 256),
        array(3, TILES, 16, LANES),
        array(2, TILES, 16, LANES),
        array(rows, LANES),
        array(rows, LANES),
    )
    motion, stress, solid, ocean, floor, *send = call(start_kernel, outs, (parity, *own, *received))
    base = coef = None
    for step in range(STEPS):
        received = exchanged(*send, "gx")
        first, last, edge = step == 0, step == STEPS - 1, step == STEPS - 2
        height = 32 if last else 24
        table = (15, TILES, height, LANES)
        scratch = [
            pltpu.VMEM((TILES, height, LANES), f32),
            pltpu.VMEM((2, 2, TILES, height, LANES), f32),
            pltpu.VMEM((3, 3, depth_cells, 256), f32),
        ]
        rows = payload_rows(slabs, "last" if edge else "usual")
        outs = (*state, array(3, TILES, 16, LANES), array(rows, LANES), array(rows, LANES))
        fixed = (motion, stress, solid, ocean, floor)
        if first:
            base = received
            inputs = (parity, *base, *fixed)
            outs = (*outs, array(*table))
        elif last:
            inputs = (parity, *base, *received, *fixed)
            scratch = [pltpu.VMEM(table, f32), *scratch]
            outs = (
                array(3, 2, depth_cells, LANES),
                array(6, 2, depth_cells, LANES),
                array(16, 8 * LANES),
                array(2, 16, 8 * LANES),
            )
        else:
            inputs = (parity, *base, *received, *fixed, coef)
        kernel = functools.partial(step_kernel, last, first, edge)
        results = call(kernel, outs, inputs, scratch)
        if first:
            coef = results[-1]
        if not last:
            motion, stress, ocean, *send = results[:5]
    return results


def solution(mesh):
    return jax.shard_map(
        body,
        mesh=mesh,
        in_specs=(
            P(None, "gx", None, "gy"),
            P(None, "gx", None, "gy"),
            P("gx", None, "gy"),
            P("gx", None, "gy"),
            P("gx", None, "gy"),
            P("gx", "gy"),
            P(None, "gx", "gy"),
            P("gx", "gy"),
            P("gx", "gy"),
        ),
        out_specs=(
            P(None, "gx", None, "gy"),
            P(None, "gx", None, "gy"),
            P("gx", "gy"),
            P(None, "gx", "gy"),
        ),
        check_vma=False,
    )
```

```python
import functools

import jax
import jax.numpy as jnp
from jax import lax
from jax.experimental import pallas as pl
from jax.experimental.pallas import tpu as pltpu
from jax.sharding import PartitionSpec as P

STEPS = 4
NSUB = 4
SOLID_STEP = 0.2
WAVE_STEP = 0.1
VISCOSITY = 0.05
UPLIFT_GAIN = 0.25
LOAD_GAIN = 8.0

INTERPRET = False
VMEM_LIMIT = 20 << 20
LANES = 128
TILES = 9
UNITS = 3 * TILES
FLOOR_UNITS = 2 * TILES


def iota(shape, dim):
    return lax.broadcasted_iota(jnp.int32, shape, dim)


def roll(value, shift, axis):
    shift = shift % value.shape[axis]
    return value if shift == 0 else pltpu.roll(value, shift, axis)


def prev_lane(value):
    return roll(value, 1, 1)


def next_lane(value):
    return roll(value, -1, 1)


def below(get, k):
    current = roll(get(k), 1, 0)
    other = roll(get(k - 1), 1, 0) if k > 0 else jnp.zeros_like(current)
    return jnp.where(iota(current.shape, 0) == 0, other, current)


def above(get, k, slabs):
    current = roll(get(k), -1, 0)
    other = roll(get(k + 1), -1, 0) if k < slabs - 1 else jnp.zeros_like(current)
    return jnp.where(iota(current.shape, 0) == 7, other, current)


def expander():
    shape = (LANES, LANES)
    return jnp.where(iota(shape, 0) == iota(shape, 1) >> 3, 1.0, 0.0)


def reducer():
    shape = (LANES, LANES)
    return jnp.where(iota(shape, 0) >> 3 == iota(shape, 1), 1.0 / 64.0, 0.0)


def exact_dot(left, right):
    return jnp.dot(
        left, right, precision=lax.Precision.HIGHEST, preferred_element_type=jnp.float32
    )


def upsampled(rows):
    lane, line = iota((8, LANES), 1), iota((8, LANES), 0)
    stack = []
    for row in rows:
        own = jnp.broadcast_to(row[:, :LANES], (8, LANES))
        halo = jnp.broadcast_to(row[:, LANES:], (8, LANES))
        tiles = own
        for t in range(1, 8):
            tiles = jnp.where(line == t, roll(own, -16 * t, 1), tiles)
        stack += [tiles, jnp.where(lane < 4, halo, roll(halo, 16, 1))]
    spread = exact_dot(jnp.concatenate(stack, axis=0), expander())
    return [spread[16 * i : 16 * i + 16] for i in range(len(rows))]


def block_means(sums):
    lane, line = iota((8, LANES), 1), iota((8, LANES), 0)
    stack = []
    for tiles in sums:
        wide = [jnp.broadcast_to(tile, (8, LANES)) for tile in tiles]
        own = wide[0]
        for t in range(1, 8):
            own = jnp.where(line == t, wide[t], own)
        stack += [own, wide[8]]
    mean = exact_dot(jnp.concatenate(stack, axis=0), reducer())
    rows = []
    for i in range(len(sums)):
        tiles, last = mean[16 * i : 16 * i + 8], mean[16 * i + 8 : 16 * i + 16]
        own = jnp.zeros((8, LANES), jnp.float32)
        for t in range(8):
            own = jnp.where((line == t) & (lane >> 4 == t), roll(tiles, 16 * t, 1), own)
        own = jnp.sum(own, axis=0, keepdims=True)
        halo = jnp.where(lane < 4, last, jnp.where(lane >= 124, roll(last, 112, 1), 0.0))
        rows.append(jnp.concatenate([own, halo[0:1]], axis=1))
    return rows


class Sender:
    def __init__(self, even, first_ref, second_ref):
        self.even, self.first, self.second = even, first_ref, second_ref

    def put(self, at, right, left):
        end = at + right.shape[0]
        self.first[at:end, :] = jnp.where(self.even, right, left)
        self.second[at:end, :] = jnp.where(self.even, left, right)

    def put_solid(self, at, slabs, right, left):
        lane = iota((8, LANES), 1)
        tails = [jnp.zeros((8, LANES), jnp.float32) for _ in range(2)]
        for k in range(slabs):
            here = (lane >= 8 * k) & (lane < 8 * k + 8)
            values = (right(k), left(k))
            for i, value in enumerate(values):
                tails[i] = jnp.where(here, roll(value[:, LANES:], 4 + 8 * k, 1), tails[i])
            self.put(at + 8 * k, values[0][:, :LANES], values[1][:, :LANES])
        self.put(at + 8 * slabs, *tails)


    def put_halves(self, at, units):
        low = iota((8, LANES), 0) < 4
        for i in range(0, len(units), 2):
            (lower, upper), (lower2, upper2) = units[i], units[min(i + 1, len(units) - 1)]
            right = jnp.where(low, roll(upper, 4, 0), upper2)
            left = jnp.where(low, lower, roll(lower2, 4, 0))
            self.put(at + 4 * i, right, left)


class Receiver:
    def __init__(self, even, first_ref, second_ref):
        self.even, self.first, self.second = even, first_ref, second_ref

    def right(self, at):
        return jnp.where(self.even, self.first[at : at + 8, :], self.second[at : at + 8, :])

    def left(self, at):
        return jnp.where(self.even, self.second[at : at + 8, :], self.first[at : at + 8, :])

    def halves(self, at, unit):
        at = at + 8 * (unit // 2)
        near, top = self.right(at), self.left(at)
        near = roll(near, 4, 0) if unit % 2 else near
        top = top if unit % 2 else roll(top, 4, 0)
        return near, top

    def solid(self, side, at, k, slabs):
        take = self.right if side > 0 else self.left
        tail = roll(take(at + 8 * slabs), -(4 + 8 * k), 1)
        return jnp.concatenate([take(at + 8 * k), tail], axis=1)


def offsets(slabs):
    part = 8 * slabs + 8
    ocean = 3 * part
    extra = ocean + 8 * ((UNITS + 1) // 2)
    more = extra + 16
    return part, ocean, extra, more


def payload_rows(slabs, kind):
    part, _, _, more = offsets(slabs)
    return {
        "first": more + part + 8 * ((FLOOR_UNITS + TILES + 1) // 2),
        "usual": more,
        "last": more + 8 * (UNITS + FLOOR_UNITS),
    }[kind]


def finish(out, slabs, motion, stress, buoyancy, ocean, floor, mean_row, kind):
    part, ocean_at, extra_at, more_at = offsets(slabs)
    low = iota((8, LANES), 0) < 4

    def get(ref, field, row):
        return lambda k: ref[field, row, 8 * k : 8 * k + 8, :]

    def rate(row, k):
        return SOLID_STEP * buoyancy[0, row, 8 * k : 8 * k + 8, :]

    def sum_x(k):
        xx, xy, xz = (get(stress, f, 1) for f in (0, 3, 4))
        mid = xy(k)
        force = (mid - prev_lane(mid)) + (xz(k) - below(xz, k)) - xx(k)
        return get(motion, 0, 1)(k) + rate(1, k) * force

    def sum_y(k):
        xy, yy, yz = (get(stress, f, 0) for f in (3, 1, 5))
        mid = yy(k)
        force = xy(k) + (next_lane(mid) - mid) + (yz(k) - below(yz, k))
        return get(motion, 1, 0)(k) + rate(0, k) * force

    def sum_z(k):
        xz, yz, zz = (get(stress, f, 0) for f in (4, 5, 2))
        mid = yz(k)
        force = xz(k) + (mid - prev_lane(mid)) + (above(zz, k, slabs) - zz(k))
        return get(motion, 2, 0)(k) + rate(0, k) * force

    def kept(compute, field, row):
        def get_and_keep(k):
            value = compute(k)
            motion[field, row, 8 * k : 8 * k + 8, :] = value
            return value

        return get_and_keep

    (spread,) = upsampled([motion[2, 0, 0:1, :]])
    out.put_solid(0, slabs, kept(sum_x, 0, 1), kept(sum_y, 1, 0))
    out.put_solid(part, slabs, get(stress, 3, 1), kept(sum_z, 2, 0))
    out.put_solid(2 * part, slabs, get(stress, 4, 1), get(stress, 0, 0))
    for t in range(TILES):
        ocean[0, t, 8:16, :] = (
            ocean[0, t, 8:16, :] + UPLIFT_GAIN * floor[1, t, 8:16, :] * spread[t : t + 1]
        )

    def units(ref, fields):
        pairs = [(f, t) for f in range(fields) for t in range(TILES)]
        return [(ref[f, t, 0:8, :], ref[f, t, 8:16, :]) for f, t in pairs]

    out.put_halves(ocean_at, units(ocean, 3))
    top = motion[2, 1, 0:8, :]
    mean_row = jnp.zeros((8, 256), jnp.float32) if mean_row is None else mean_row
    mean_row = jnp.broadcast_to(mean_row, (8, 256))
    for i in range(2):
        lanes = slice(LANES * i, LANES * i + LANES)
        out.put(extra_at + 8 * i, top[:, lanes], mean_row[:, lanes])
    if kind == "first":
        out.put_solid(more_at, slabs, get(buoyancy, 0, 1), get(buoyancy, 0, 0))
        faces = []
        for t in range(TILES):
            wet = floor[1, t, :, :]
            faces.append(((wet * roll(wet, -1, 0))[0:8], wet[8:16]))
        out.put_halves(more_at + part, units(floor, 2) + faces)
    if kind == "last":
        for i, (lower, upper) in enumerate(units(ocean, 3) + units(floor, 2)):
            value = jnp.where(low, upper, lower)
            out.put(more_at + 8 * i, value, value)


def pack_y_kernel(
    parity, motion, stress, buoyancy, first, shear, surface, momentum, depth, wet,
    motion_out, stress_out, solid_out, ocean_out, floor_out, one, two,
    surface_in, momentum_in, depth_in, wet_in, semaphores,
):
    own = slice(0, LANES)
    pairs = [(motion, motion_out.at[:, :, :, own]), (stress, stress_out.at[:, :, :, own])]
    for f, ref in enumerate((buoyancy, first, shear)):
        pairs.append((ref, solid_out.at[f, :, :, own]))
    pairs += [(surface, surface_in), (momentum, momentum_in), (depth, depth_in), (wet, wet_in)]
    copies = [
        pltpu.make_async_copy(source, target, semaphores.at[i])
        for i, (source, target) in enumerate(pairs)
    ]
    for copy in copies:
        copy.start()
    out = Sender(parity[1] == 0, one, two)
    slabs = motion.shape[2] // 8
    lane = iota((8, LANES), 1)
    fields = [(motion_out, f, 0) for f in range(3)] + [(stress_out, f, 1) for f in range(6)]
    fields += [(solid_out, f, 2 + f) for f in range(3)]
    count, at, waited = 0, 0, set()
    right = left = jnp.zeros((8, LANES), jnp.float32)
    for ref, f, copy in fields:
        if copy not in waited:
            copies[copy].wait()
            waited.add(copy)
        for row in range(2):
            for k in range(slabs):
                value = ref[f, row, 8 * k : 8 * k + 8, own]
                here = lane >> 2 == count
                right = jnp.where(here, roll(value, 4 * count + 4, 1), right)
                left = jnp.where(here, roll(value, 4 * count, 1), left)
                count += 1
                if count == 32:
                    out.put(at, right, left)
                    count, at = 0, at + 8
    if count:
        out.put(at, right, left)
        count, at = 0, at + 8
    for copy in copies[5:]:
        copy.wait()
    targets = [ocean_out.at[f] for f in range(3)] + [floor_out.at[f] for f in range(2)]
    sources = [surface_in, momentum_in.at[0], momentum_in.at[1], depth_in, wet_in]
    for target, source in zip(targets, sources):
        for group in range(2):
            rows = slice(8 * group, 8 * group + 8)
            for t in range(TILES - 1):
                lanes = slice(LANES * t, LANES * t + LANES)
                value = source[rows, lanes].astype(jnp.float32)
                target[t, rows, :] = value
                here = lane >> 5 == count
                if t == 0:
                    left = jnp.where(here, roll(value, 32 * count, 1), left)
                if t == TILES - 2:
                    right = jnp.where(here, roll(value, 32 * count + 32, 1), right)
            count += 1
            if count == 4:
                out.put(at, right, left)
                count, at = 0, at + 8
    if count:
        out.put(at, right, left)


def pack_y_rows(slabs):
    return 8 * (-(-24 * slabs // 32) + 3)


def start_kernel(
    parity, motion_in, stress_in, solid_in, ocean_in, floor_in, one, two,
    motion, stress, solid, ocean, floor, send_one, send_two,
):
    inbox = Receiver(parity[1] == 0, one, two)
    slabs = motion.shape[2] // 8
    lane = iota((8, LANES), 1)
    fields = [(motion, f) for f in range(3)] + [(stress, f) for f in range(6)]
    fields += [(solid, f) for f in range(3)]
    count, at = 0, 0
    for ref, f in fields:
        for row in range(2):
            for k in range(slabs):
                if count == 0:
                    packed = inbox.right(at), inbox.left(at)
                after = roll(packed[0], -4 * count, 1)
                before = roll(packed[1], 124 - 4 * count, 1)
                halo = jnp.where(lane < 4, after, jnp.where(lane >= 124, before, 0.0))
                ref[f, row, 8 * k : 8 * k + 8, LANES : 2 * LANES] = halo
                count += 1
                if count == 32:
                    count, at = 0, at + 8
    if count:
        count, at = 0, at + 8
    for ref, f in [(ocean, 0), (ocean, 1), (ocean, 2), (floor, 0), (floor, 1)]:
        for group in range(2):
            if count == 0:
                packed = inbox.right(at), inbox.left(at)
            after = roll(packed[0], -32 * count, 1)
            before = roll(packed[1], 96 - 32 * count, 1)
            halo = jnp.where(lane < 32, after, jnp.where(lane >= 96, before, 0.0))
            ref[f, TILES - 1, 8 * group : 8 * group + 8, :] = halo
            count += 1
            if count == 4:
                count, at = 0, at + 8
    out = Sender(parity[0] == 0, send_one, send_two)
    finish(out, slabs, motion, stress, solid, ocean, floor, None, "first")


PAD = 8


class Shifts:
    def __init__(self, tile, by):
        self.tile, self.by, self.rolled = tile, by, {}

    def rotated(self, t):
        if t not in self.rolled:
            self.rolled[t] = roll(self.tile(t), self.by, 1)
        return self.rolled[t]

    def at(self, t):
        lane = iota((8, LANES), 1)
        other, mine = self.rotated((t - self.by) % TILES), self.rotated(t)
        return jnp.where(lane == (0 if self.by > 0 else LANES - 1), other, mine)


def coefficients(coef, face, depth, after):
    groups = coef.shape[2] // 8
    for t in range(TILES):
        for g in range(groups):
            at = PAD + 8 * g
            wet = face[0, t, at : at + 8, :]
            coef[7, t, 8 * g : 8 * g + 8, :] = wet
            coef[0, t, 8 * g : 8 * g + 8, :] = WAVE_STEP * wet
    for direction in range(2):
        for g in range(groups):
            at = PAD + 8 * g
            wets = Shifts(lambda t: coef[7, t, 8 * g : 8 * g + 8, :], -1)
            depths = Shifts(lambda t: depth[t, at : at + 8, :], -1)
            for t in range(TILES):
                wet = wets.tile(t)
                here = depths.tile(t)
                if direction == 0:
                    beside = face[0, t, at + 1 : at + 9, :]
                    deep = depth[t, at + 1 : at + 9, :]
                else:
                    beside, deep = wets.at(t), depths.at(t)
                face[1, t, at : at + 8, :] = wet * beside
                coef[3 + 3 * direction, t, 8 * g : 8 * g + 8, :] = here + deep
        if direction == 0 and after is not None:
            for t in range(TILES):
                face[1, t, PAD + 20 : PAD + 28, :] = after(t)
        for g in range(groups):
            at = PAD + 8 * g
            ahead = Shifts(lambda t: face[1, t, at : at + 8, :], -1)
            behind = Shifts(ahead.tile, 1)
            for t in range(TILES):
                own = ahead.tile(t)
                total = face[1, t, at - 1 : at + 7, :] + face[1, t, at + 1 : at + 9, :]
                total = total + ahead.at(t) + behind.at(t)
                rows = slice(8 * g, 8 * g + 8)
                coef[1 + 3 * direction, t, rows, :] = VISCOSITY * own
                coef[2 + 3 * direction, t, rows, :] = own - VISCOSITY * own * total


def ocean_part(
    inbox, base, slabs, motion, ocean, floor, wide, first, coef, height, flow, side, row_left
):
    part, ocean_at, _, more_at = offsets(slabs)
    low = iota((8, LANES), 0) < 4
    groups = 4 if wide else 3

    def place(target, t, own, near, top, far):
        target[t, PAD - 4 : PAD + 4, :] = top
        target[t, PAD + 4 : PAD + 20, :] = own
        if wide:
            near = jnp.where(low, near, far)
            target[t, PAD + 28 : PAD + 36, :] = far
        target[t, PAD + 20 : PAD + 28, :] = near

    if first or wide:
        for t in range(TILES):
            for f, target in ((1, flow.at[0, 0]), (0, height)):
                near, top = base.halves(more_at + part, f * TILES + t)
                far = inbox.right(more_at + 8 * (UNITS + f * TILES + t)) if wide else None
                place(target, t, floor[f, t, :, :], near, top, far)
        after = lambda t: base.halves(more_at + part, 2 * TILES + t)[0]
        coefficients(coef, flow.at[0], height, None if wide else after)
    spread_left, spread_last = upsampled([row_left, motion[2, 1, 0:1, :]])
    for t in range(TILES):
        for f in range(3):
            near, top = inbox.halves(ocean_at, f * TILES + t)
            far = inbox.right(more_at + 8 * (f * TILES + t)) if wide else None
            target = height if f == 0 else flow.at[0, f - 1]
            place(target, t, ocean[f, t, :, :], near, top, far)
        for g in range(groups):
            spread = spread_left if g < 2 else spread_last
            lift = UPLIFT_GAIN * coef[7, t, 8 * g : 8 * g + 8, :] * spread[t : t + 1]
            lift = jnp.where(low == (g % 2 == 1), lift, 0.0)
            at = PAD + 8 * g
            height[t, at : at + 8, :] = height[t, at : at + 8, :] + lift
    for step in range(NSUB):
        old, new = step % 2, (step + 1) % 2
        for g in range(groups):
            at, rows = PAD + 8 * g, slice(8 * g, 8 * g + 8)
            n_behind = Shifts(lambda t: flow[old, 1, t, at : at + 8, :], 1)
            for t in range(TILES):
                m, n = flow[old, 0, t, at : at + 8, :], n_behind.tile(t)
                west = n_behind.at(t)
                if not (first and step == 0):
                    side[t, rows, :] = west
                spill = (m - flow[old, 0, t, at - 1 : at + 7, :]) + (n - west)
                height[t, at : at + 8, :] = height[t, at : at + 8, :] - coef[0, t, rows, :] * spill
        if first and step == 0:
            for t in range(TILES):
                for g in range(groups):
                    at, rows = PAD + 8 * g, slice(8 * g, 8 * g + 8)
                    for d in range(2):
                        wet = jnp.where(coef[1 + 3 * d, t, rows, :] > 0.0, 1.0, 0.0)
                        flow[old, d, t, at : at + 8, :] = wet * flow[old, d, t, at : at + 8, :]
        for g in range(groups):
            at, rows = PAD + 8 * g, slice(8 * g, 8 * g + 8)
            h_ahead = Shifts(lambda t: height[t, at : at + 8, :], -1)
            ahead = [Shifts(lambda t, d=d: flow[old, d, t, at : at + 8, :], -1) for d in range(2)]
            m_behind = Shifts(ahead[0].tile, 1)
            n_behind = Shifts(ahead[1].tile, 1)
            for t in range(TILES):
                h = height[t, at : at + 8, :]
                sides = [height[t, at + 1 : at + 9, :], h_ahead.at(t)]
                for d in range(2):
                    q = flow[old, d, t, at : at + 8, :]
                    around = flow[old, d, t, at - 1 : at + 7, :] + flow[old, d, t, at + 1 : at + 9, :]
                    around = around + ahead[d].at(t)
                    if d == 0:
                        around = around + m_behind.at(t)
                    elif first and step == 0:
                        around = around + n_behind.at(t)
                    else:
                        around = around + side[t, rows, :]
                    c = 1 + 3 * d
                    slope = (coef[c + 2, t, rows, :] + h + sides[d]) * (sides[d] - h)
                    value = coef[c + 1, t, rows, :] * q + coef[c, t, rows, :] * (around - slope)
                    flow[new, d, t, at : at + 8, :] = value


def step_kernel(last, is_first, edge, *refs):
    parity, refs = refs[0], list(refs[1:])

    def take(count):
        taken = refs[:count]
        del refs[:count]
        return taken

    base_one, base_two = take(2)
    one, two = (base_one, base_two) if is_first else take(2)
    motion, stress, solid, ocean, floor = take(5)
    ready = not (is_first or last)
    if ready:
        (coef,) = take(1)
    if last:
        motion_out, stress_out, surface_out, momentum_out = take(4)
    else:
        motion_out, stress_out, ocean_out, send_one, send_two = take(5)
    if not ready:
        (coef,) = take(1)
    height, flow, side, speed = take(4)
    slabs = motion.shape[2] // 8
    part, _, extra_at, more_at = offsets(slabs)
    even = parity[0] == 0
    base = Receiver(even, base_one, base_two)
    inbox = Receiver(even, one, two)

    def extra_row(take):
        return jnp.concatenate([take(extra_at)[0:1], take(extra_at + 8)[0:1]], axis=1)

    row_left = extra_row(inbox.left)
    loaded = None if is_first else -LOAD_GAIN * extra_row(inbox.right)
    ocean_part(
        inbox, base, slabs, motion, ocean, floor, last, is_first, coef, height, flow, side, row_left
    )
    blocks = 3 if last else 2
    sums = [[] for _ in range(blocks)]
    rows = slice(PAD + 4, PAD + 20)
    for t in range(TILES):
        for b in range(blocks):
            at = 8 * b + 4
            wet = coef[7, t, at : at + 8, :]
            h = height[t, PAD + at : PAD + at + 8, :]
            sums[b].append(jnp.sum(wet * h, axis=0, keepdims=True))
        if last:
            if t < TILES - 1:
                lanes = slice(LANES * t, LANES * t + LANES)
                surface_out[:, lanes] = height[t, rows, :]
                for d in range(2):
                    momentum_out[d, :, lanes] = flow[NSUB % 2, d, t, rows, :]
        else:
            ocean_out[0, t] = height[t, rows, :]
            for d in range(2):
                ocean_out[1 + d, t] = flow[NSUB % 2, d, t, rows, :]
    means = block_means(sums)

    def old(f, row):
        def get(k):
            value = stress[f, row, 8 * k : 8 * k + 8, :]
            if (f, row, k) == (2, 1, 0) and loaded is not None:
                value = jnp.where(iota(value.shape, 0) == 0, loaded, value)
            return value

        return get

    def new(f, row):
        return lambda k: speed[f, row, 8 * k : 8 * k + 8, :]

    for k in range(slabs):
        z = slice(8 * k, 8 * k + 8)
        xx = [stress[0, 0, z, :], stress[0, 1, z, :], inbox.solid(1, 2 * part, k, slabs)]
        xy = [inbox.solid(-1, part, k, slabs), stress[3, 0, z, :], stress[3, 1, z, :]]
        xz = [inbox.solid(-1, 2 * part, k, slabs), stress[4, 0, z, :], stress[4, 1, z, :]]
        rate_left = SOLID_STEP * base.solid(-1, more_at, k, slabs)
        rate_right = SOLID_STEP * base.solid(1, more_at, k, slabs)
        speed[0, 2, z, :] = inbox.solid(-1, 0, k, slabs) + rate_left * xx[0]
        speed[1, 2, z, :] = inbox.solid(1, 0, k, slabs) - rate_right * xy[2]
        speed[2, 2, z, :] = inbox.solid(1, part, k, slabs) - rate_right * xz[2]
        rates = [SOLID_STEP * solid[0, row, z, :] for row in range(2)]
        whole_x = (xx[1] - xx[0]) + (xy[1] - prev_lane(xy[1])) + (xz[1] - below(old(4, 0), k))
        yy, zz, yz = stress[1, 1, z, :], old(2, 1), stress[5, 1, z, :]
        whole_y = (xy[2] - xy[1]) + (next_lane(yy) - yy) + (yz - below(old(5, 1), k))
        whole_z = (xz[2] - xz[1]) + (yz - prev_lane(yz)) + (above(zz, k, slabs) - zz(k))
        forces = {
            (0, 0): whole_x, (0, 1): xx[2],
            (1, 0): -xy[0], (1, 1): whole_y,
            (2, 0): -xz[0], (2, 1): whole_z,
        }
        for (f, row), force in forces.items():
            value = motion[f, row, z, :] + rates[row] * force
            speed[f, row, z, :] = value
            motion_out[f, row, z, :] = value[:, :LANES] if last else value
    width = LANES if last else 2 * LANES
    for k in range(slabs):
        z = slice(8 * k, 8 * k + 8)
        x_of = [speed[0, 2, z, :], speed[0, 0, z, :], speed[0, 1, z, :]]
        y_of = [speed[1, 0, z, :], speed[1, 1, z, :], speed[1, 2, z, :]]
        z_of = [speed[2, 0, z, :], speed[2, 1, z, :], speed[2, 2, z, :]]
        for row in range(2):
            vx, vy, vz = x_of[row + 1], y_of[row], z_of[row]
            strain_x = vx - x_of[row]
            strain_y = vy - prev_lane(vy)
            strain_z = vz - below(new(2, row), k)
            shear = SOLID_STEP * solid[2, row, z, :]
            lame = SOLID_STEP * solid[1, row, z, :]
            common = lame * (strain_x + strain_y + strain_z)
            twice = shear + shear
            rates = [common + twice * strain for strain in (strain_x, strain_y, strain_z)]
            rates.append(shear * ((next_lane(vx) - vx) + (y_of[row + 1] - vy)))
            rates.append(shear * ((above(new(0, row), k, slabs) - vx) + (z_of[row + 1] - vz)))
            rates.append(shear * ((above(new(1, row), k, slabs) - vy) + (next_lane(vz) - vz)))
            for f in range(6):
                value = stress[f, row, z, :] + rates[f]
                stress_out[f, row, z, :] = value[:, :width]
    stress_out[2, 0, 0:1, :] = -LOAD_GAIN * means[1][:, :width]
    if last:
        stress_out[2, 1, 0:1, :] = -LOAD_GAIN * means[2][:, :width]
        return
    out = Sender(even, send_one, send_two)
    next_kind = "last" if edge else "usual"
    finish(out, slabs, motion_out, stress_out, solid, ocean_out, floor, means[0], next_kind)


def swap(size, start):
    pairs = []
    for i in range(start, size - 1, 2):
        pairs += [(i, i + 1), (i + 1, i)]
    return pairs


def exchanged(first, second, axis):
    size = lax.axis_size(axis)
    return (
        lax.ppermute(first, axis, swap(size, 0)),
        lax.ppermute(second, axis, swap(size, 1)),
    )


def body(motion, stress, buoyancy, lame_first, lame_shear, surface, momentum, bathymetry, wet_mask):
    depth_cells = motion.shape[2]
    slabs = depth_cells // 8
    f32 = jnp.float32

    def array(*shape):
        return jax.ShapeDtypeStruct(shape, f32)

    def call(kernel, outs, args, scratch=(), space=pltpu.VMEM, aliases=None):
        specs = [pl.BlockSpec(memory_space=pltpu.SMEM)]
        specs += [pl.BlockSpec(memory_space=space)] * (len(args) - 1)
        return pl.pallas_call(
            kernel,
            out_shape=outs,
            in_specs=specs,
            out_specs=tuple(pl.BlockSpec(memory_space=pltpu.VMEM) for _ in outs),
            scratch_shapes=list(scratch),
            input_output_aliases=aliases or {},
            compiler_params=pltpu.CompilerParams(vmem_limit_bytes=VMEM_LIMIT),
            interpret=INTERPRET,
        )(*args)

    parity = jnp.stack([lax.axis_index("gx") % 2, lax.axis_index("gy") % 2]).astype(jnp.int32)
    own = (
        motion, stress, buoyancy, lame_first, lame_shear, surface, momentum, bathymetry, wet_mask,
    )
    state = (array(3, 2, depth_cells, 256), array(6, 2, depth_cells, 256))
    wide = (
        *state,
        array(3, 2, depth_cells, 256),
        array(3, TILES, 16, LANES),
        array(2, TILES, 16, LANES),
    )
    scratch = [pltpu.VMEM(x.shape, x.dtype) for x in (surface, momentum, bathymetry, wet_mask)]
    scratch.append(pltpu.SemaphoreType.DMA((len(own),)))
    packed = (array(pack_y_rows(slabs), LANES),) * 2
    *held, one, two = call(pack_y_kernel, (*wide, *packed), (parity, *own), scratch, pltpu.HBM)
    received = exchanged(one, two, "gy")
    packed = (array(payload_rows(slabs, "first"), LANES),) * 2
    motion, stress, solid, ocean, floor, *send = call(
        start_kernel, (*wide, *packed), (parity, *held, *received), aliases={i + 1: i for i in range(5)}
    )
    base = coef = None
    for step in range(STEPS):
        received = exchanged(*send, "gx")
        first, last, edge = step == 0, step == STEPS - 1, step == STEPS - 2
        height = 32 if last else 24
        table = (8, TILES, height, LANES)
        padded = height + 2 * PAD
        scratch = [
            pltpu.VMEM((TILES, padded, LANES), f32),
            pltpu.VMEM((2, 2, TILES, padded, LANES), f32),
            pltpu.VMEM((TILES, height, LANES), f32),
            pltpu.VMEM((3, 3, depth_cells, 256), f32),
        ]
        rows = payload_rows(slabs, "last" if edge else "usual")
        outs = (*state, array(3, TILES, 16, LANES), array(rows, LANES), array(rows, LANES))
        fixed = (motion, stress, solid, ocean, floor)
        if first:
            base = received
            inputs = (parity, *base, *fixed)
            outs = (*outs, array(*table))
        elif last:
            inputs = (parity, *base, *received, *fixed)
            scratch = [pltpu.VMEM(table, f32), *scratch]
            outs = (
                array(3, 2, depth_cells, LANES),
                array(6, 2, depth_cells, LANES),
                array(16, 8 * LANES),
                array(2, 16, 8 * LANES),
            )
        else:
            inputs = (parity, *base, *received, *fixed, coef)
        kernel = functools.partial(step_kernel, last, first, edge)
        results = call(kernel, outs, inputs, scratch)
        if first:
            coef = results[-1]
        if not last:
            motion, stress, ocean, *send = results[:5]
    return results


def solution(mesh):
    return jax.shard_map(
        body,
        mesh=mesh,
        in_specs=(
            P(None, "gx", None, "gy"),
            P(None, "gx", None, "gy"),
            P("gx", None, "gy"),
            P("gx", None, "gy"),
            P("gx", None, "gy"),
            P("gx", "gy"),
            P(None, "gx", "gy"),
            P("gx", "gy"),
            P("gx", "gy"),
        ),
        out_specs=(
            P(None, "gx", None, "gy"),
            P(None, "gx", None, "gy"),
            P("gx", "gy"),
            P(None, "gx", "gy"),
        ),
        check_vma=False,
    )
```

```python
import functools

import jax
import jax.numpy as jnp
from jax import lax
from jax.experimental import pallas as pl
from jax.experimental.pallas import tpu as pltpu
from jax.sharding import PartitionSpec as P

STEPS = 4
NSUB = 4
SOLID_STEP = 0.2
WAVE_STEP = 0.1
VISCOSITY = 0.05
UPLIFT_GAIN = 0.25
LOAD_GAIN = 8.0

INTERPRET = False
VMEM_LIMIT = 20 << 20
LOADER_LIMIT = 62_000_000
LANES = 128
TILES = 9
UNITS = 3 * TILES
FLOOR_UNITS = 2 * TILES


def iota(shape, dim):
    return lax.broadcasted_iota(jnp.int32, shape, dim)


def roll(value, shift, axis):
    shift = shift % value.shape[axis]
    return value if shift == 0 else pltpu.roll(value, shift, axis)


def prev_lane(value):
    return roll(value, 1, 1)


def next_lane(value):
    return roll(value, -1, 1)


def below(get, k):
    current = roll(get(k), 1, 0)
    other = roll(get(k - 1), 1, 0) if k > 0 else jnp.zeros_like(current)
    return jnp.where(iota(current.shape, 0) == 0, other, current)


def above(get, k, slabs):
    current = roll(get(k), -1, 0)
    other = roll(get(k + 1), -1, 0) if k < slabs - 1 else jnp.zeros_like(current)
    return jnp.where(iota(current.shape, 0) == 7, other, current)


def expander():
    shape = (LANES, LANES)
    return jnp.where(iota(shape, 0) == iota(shape, 1) >> 3, 1.0, 0.0)


def reducer():
    shape = (LANES, LANES)
    return jnp.where(iota(shape, 0) >> 3 == iota(shape, 1), 1.0 / 64.0, 0.0)


def exact_dot(left, right):
    return jnp.dot(
        left, right, precision=lax.Precision.HIGHEST, preferred_element_type=jnp.float32
    )


def upsampled(rows):
    lane, line = iota((8, LANES), 1), iota((8, LANES), 0)
    stack = []
    for row in rows:
        own = jnp.broadcast_to(row[:, :LANES], (8, LANES))
        halo = jnp.broadcast_to(row[:, LANES:], (8, LANES))
        tiles = own
        for t in range(1, 8):
            tiles = jnp.where(line == t, roll(own, -16 * t, 1), tiles)
        stack += [tiles, jnp.where(lane < 4, halo, roll(halo, 16, 1))]
    spread = exact_dot(jnp.concatenate(stack, axis=0), expander())
    return [spread[16 * i : 16 * i + 16] for i in range(len(rows))]


def block_means(sums):
    lane, line = iota((8, LANES), 1), iota((8, LANES), 0)
    stack = []
    for tiles in sums:
        wide = [jnp.broadcast_to(tile, (8, LANES)) for tile in tiles]
        own = wide[0]
        for t in range(1, 8):
            own = jnp.where(line == t, wide[t], own)
        stack += [own, wide[8]]
    mean = exact_dot(jnp.concatenate(stack, axis=0), reducer())
    rows = []
    for i in range(len(sums)):
        tiles, last = mean[16 * i : 16 * i + 8], mean[16 * i + 8 : 16 * i + 16]
        own = jnp.zeros((8, LANES), jnp.float32)
        for t in range(8):
            own = jnp.where((line == t) & (lane >> 4 == t), roll(tiles, 16 * t, 1), own)
        own = jnp.sum(own, axis=0, keepdims=True)
        halo = jnp.where(lane < 4, last, jnp.where(lane >= 124, roll(last, 112, 1), 0.0))
        rows.append(jnp.concatenate([own, halo[0:1]], axis=1))
    return rows


class Sender:
    def __init__(self, even, first_ref, second_ref):
        self.even, self.first, self.second = even, first_ref, second_ref

    def put(self, at, right, left):
        end = at + right.shape[0]
        self.first[at:end, :] = jnp.where(self.even, right, left)
        self.second[at:end, :] = jnp.where(self.even, left, right)

    def put_solid(self, at, slabs, right, left):
        lane = iota((8, LANES), 1)
        tails = [jnp.zeros((8, LANES), jnp.float32) for _ in range(2)]
        for k in range(slabs):
            here = (lane >= 8 * k) & (lane < 8 * k + 8)
            values = (right(k), left(k))
            for i, value in enumerate(values):
                tails[i] = jnp.where(here, roll(value[:, LANES:], 4 + 8 * k, 1), tails[i])
            self.put(at + 8 * k, values[0][:, :LANES], values[1][:, :LANES])
        self.put(at + 8 * slabs, *tails)


    def put_halves(self, at, units):
        low = iota((8, LANES), 0) < 4
        for i in range(0, len(units), 2):
            (lower, upper), (lower2, upper2) = units[i], units[min(i + 1, len(units) - 1)]
            right = jnp.where(low, roll(upper, 4, 0), upper2)
            left = jnp.where(low, lower, roll(lower2, 4, 0))
            self.put(at + 4 * i, right, left)


class Receiver:
    def __init__(self, even, first_ref, second_ref):
        self.even, self.first, self.second = even, first_ref, second_ref

    def right(self, at):
        return jnp.where(self.even, self.first[at : at + 8, :], self.second[at : at + 8, :])

    def left(self, at):
        return jnp.where(self.even, self.second[at : at + 8, :], self.first[at : at + 8, :])

    def halves(self, at, unit):
        at = at + 8 * (unit // 2)
        near, top = self.right(at), self.left(at)
        near = roll(near, 4, 0) if unit % 2 else near
        top = top if unit % 2 else roll(top, 4, 0)
        return near, top

    def solid(self, side, at, k, slabs):
        take = self.right if side > 0 else self.left
        tail = roll(take(at + 8 * slabs), -(4 + 8 * k), 1)
        return jnp.concatenate([take(at + 8 * k), tail], axis=1)


def offsets(slabs):
    part = 8 * slabs + 8
    ocean = 3 * part
    extra = ocean + 8 * ((UNITS + 1) // 2)
    more = extra + 16
    return part, ocean, extra, more


def payload_rows(slabs, kind):
    part, _, _, more = offsets(slabs)
    return {
        "first": more + part + 8 * ((FLOOR_UNITS + TILES + 1) // 2),
        "usual": more,
        "last": more + 8 * (UNITS + FLOOR_UNITS),
    }[kind]


def finish(out, slabs, motion, stress, buoyancy, ocean, floor, mean_row, kind):
    part, ocean_at, extra_at, more_at = offsets(slabs)
    low = iota((8, LANES), 0) < 4

    def get(ref, field, row):
        return lambda k: ref[field, row, 8 * k : 8 * k + 8, :]

    def rate(row, k):
        return SOLID_STEP * buoyancy[0, row, 8 * k : 8 * k + 8, :]

    def sum_x(k):
        xx, xy, xz = (get(stress, f, 1) for f in (0, 3, 4))
        mid = xy(k)
        force = (mid - prev_lane(mid)) + (xz(k) - below(xz, k)) - xx(k)
        return get(motion, 0, 1)(k) + rate(1, k) * force

    def sum_y(k):
        xy, yy, yz = (get(stress, f, 0) for f in (3, 1, 5))
        mid = yy(k)
        force = xy(k) + (next_lane(mid) - mid) + (yz(k) - below(yz, k))
        return get(motion, 1, 0)(k) + rate(0, k) * force

    def sum_z(k):
        xz, yz, zz = (get(stress, f, 0) for f in (4, 5, 2))
        mid = yz(k)
        force = xz(k) + (mid - prev_lane(mid)) + (above(zz, k, slabs) - zz(k))
        return get(motion, 2, 0)(k) + rate(0, k) * force

    def kept(compute, field, row):
        def get_and_keep(k):
            value = compute(k)
            motion[field, row, 8 * k : 8 * k + 8, :] = value
            return value

        return get_and_keep

    (spread,) = upsampled([motion[2, 0, 0:1, :]])
    out.put_solid(0, slabs, kept(sum_x, 0, 1), kept(sum_y, 1, 0))
    out.put_solid(part, slabs, get(stress, 3, 1), kept(sum_z, 2, 0))
    out.put_solid(2 * part, slabs, get(stress, 4, 1), get(stress, 0, 0))
    for t in range(TILES):
        ocean[0, t, 8:16, :] = (
            ocean[0, t, 8:16, :] + UPLIFT_GAIN * floor[1, t, 8:16, :] * spread[t : t + 1]
        )

    def units(ref, fields):
        pairs = [(f, t) for f in range(fields) for t in range(TILES)]
        return [(ref[f, t, 0:8, :], ref[f, t, 8:16, :]) for f, t in pairs]

    out.put_halves(ocean_at, units(ocean, 3))
    top = motion[2, 1, 0:8, :]
    mean_row = jnp.zeros((8, 256), jnp.float32) if mean_row is None else mean_row
    mean_row = jnp.broadcast_to(mean_row, (8, 256))
    for i in range(2):
        lanes = slice(LANES * i, LANES * i + LANES)
        out.put(extra_at + 8 * i, top[:, lanes], mean_row[:, lanes])
    if kind == "first":
        out.put_solid(more_at, slabs, get(buoyancy, 0, 1), get(buoyancy, 0, 0))
        faces = []
        for t in range(TILES):
            wet = floor[1, t, :, :]
            faces.append(((wet * roll(wet, -1, 0))[0:8], wet[8:16]))
        out.put_halves(more_at + part, units(floor, 2) + faces)
    if kind == "last":
        for i, (lower, upper) in enumerate(units(ocean, 3) + units(floor, 2)):
            value = jnp.where(low, upper, lower)
            out.put(more_at + 8 * i, value, value)


def pack_y_kernel(
    parity, motion, stress, buoyancy, first, shear, surface, momentum, depth, wet, one, two
):
    even = parity[1] == 0
    out = Sender(even, one, two)
    slabs = motion.shape[2] // 8
    lane = iota((8, LANES), 1)
    fields = [(motion, f) for f in range(3)] + [(stress, f) for f in range(6)]
    fields += [(buoyancy, None), (first, None), (shear, None)]
    count, at = 0, 0
    right = left = jnp.zeros((8, LANES), jnp.float32)
    for ref, f in fields:
        for row in range(2):
            for k in range(slabs):
                z = slice(8 * k, 8 * k + 8)
                value = ref[row, z, :] if f is None else ref[f, row, z, :]
                here = lane >> 2 == count
                right = jnp.where(here, roll(value, 4 * count + 4, 1), right)
                left = jnp.where(here, roll(value, 4 * count, 1), left)
                count += 1
                if count == 32:
                    out.put(at, right, left)
                    count, at = 0, at + 8
    if count:
        out.put(at, right, left)
        count, at = 0, at + 8
    width = surface.shape[1]
    for ref, f in ((surface, None), (momentum, 0), (momentum, 1), (depth, None), (wet, None)):
        for group in range(2):
            rows = slice(8 * group, 8 * group + 8)
            ends = []
            for lanes in (slice(0, LANES), slice(width - LANES, width)):
                value = ref[rows, lanes] if f is None else ref[f, rows, lanes]
                ends.append(value.astype(jnp.float32))
            here = lane >> 5 == count
            right = jnp.where(here, roll(ends[1], 32 * count + 32, 1), right)
            left = jnp.where(here, roll(ends[0], 32 * count, 1), left)
            count += 1
            if count == 4:
                out.put(at, right, left)
                count, at = 0, at + 8
    if count:
        out.put(at, right, left)


def pack_y_rows(slabs):
    return 8 * (-(-24 * slabs // 32) + 3)


def start_kernel(
    parity, motion, stress, buoyancy, first, shear, surface, momentum, depth, wet, one, two,
    motion_out, stress_out, solid_out, ocean_out, floor_out, send_one, send_two,
):
    inbox = Receiver(parity[1] == 0, one, two)
    slabs = motion.shape[2] // 8
    lane = iota((8, LANES), 1)
    fields = [(motion, f, motion_out, f) for f in range(3)]
    fields += [(stress, f, stress_out, f) for f in range(6)]
    fields += [(ref, None, solid_out, f) for f, ref in enumerate((buoyancy, first, shear))]
    count, at = 0, 0
    for ref, f, target, g in fields:
        for row in range(2):
            for k in range(slabs):
                z = slice(8 * k, 8 * k + 8)
                value = ref[row, z, :] if f is None else ref[f, row, z, :]
                if count == 0:
                    packed = inbox.right(at), inbox.left(at)
                after = roll(packed[0], -4 * count, 1)
                before = roll(packed[1], 124 - 4 * count, 1)
                halo = jnp.where(lane < 4, after, jnp.where(lane >= 124, before, 0.0))
                target[g, row, z, 0:LANES] = value
                target[g, row, z, LANES : 2 * LANES] = halo
                count += 1
                if count == 32:
                    count, at = 0, at + 8
    if count:
        count, at = 0, at + 8
    targets = ((surface, None), (momentum, 0), (momentum, 1), (depth, None), (wet, None))
    for i, (ref, f) in enumerate(targets):
        for group in range(2):
            rows = slice(8 * group, 8 * group + 8)
            if count == 0:
                packed = inbox.right(at), inbox.left(at)
            after = roll(packed[0], -32 * count, 1)
            before = roll(packed[1], 96 - 32 * count, 1)
            halo = jnp.where(lane < 32, after, jnp.where(lane >= 96, before, 0.0))
            for t in range(TILES):
                if t == TILES - 1:
                    value = halo
                else:
                    lanes = slice(LANES * t, LANES * t + LANES)
                    value = ref[rows, lanes] if f is None else ref[f, rows, lanes]
                    value = value.astype(jnp.float32)
                if i < 3:
                    ocean_out[i, t, rows, :] = value
                else:
                    floor_out[i - 3, t, rows, :] = value
            count += 1
            if count == 4:
                count, at = 0, at + 8
    out = Sender(parity[0] == 0, send_one, send_two)
    finish(out, slabs, motion_out, stress_out, solid_out, ocean_out, floor_out, None, "first")


PAD = 8


class Shifts:
    def __init__(self, tile, by):
        self.tile, self.by, self.rolled = tile, by, {}

    def rotated(self, t):
        if t not in self.rolled:
            self.rolled[t] = roll(self.tile(t), self.by, 1)
        return self.rolled[t]

    def at(self, t):
        lane = iota((8, LANES), 1)
        other, mine = self.rotated((t - self.by) % TILES), self.rotated(t)
        return jnp.where(lane == (0 if self.by > 0 else LANES - 1), other, mine)


def coefficients(coef, face, depth, after):
    groups = coef.shape[2] // 8
    for t in range(TILES):
        for g in range(groups):
            at = PAD + 8 * g
            wet = face[0, t, at : at + 8, :]
            coef[7, t, 8 * g : 8 * g + 8, :] = wet
            coef[0, t, 8 * g : 8 * g + 8, :] = WAVE_STEP * wet
    for direction in range(2):
        for g in range(groups):
            at = PAD + 8 * g
            wets = Shifts(lambda t: coef[7, t, 8 * g : 8 * g + 8, :], -1)
            depths = Shifts(lambda t: depth[t, at : at + 8, :], -1)
            for t in range(TILES):
                wet = wets.tile(t)
                here = depths.tile(t)
                if direction == 0:
                    beside = face[0, t, at + 1 : at + 9, :]
                    deep = depth[t, at + 1 : at + 9, :]
                else:
                    beside, deep = wets.at(t), depths.at(t)
                face[1, t, at : at + 8, :] = wet * beside
                coef[3 + 3 * direction, t, 8 * g : 8 * g + 8, :] = here + deep
        if direction == 0 and after is not None:
            for t in range(TILES):
                face[1, t, PAD + 20 : PAD + 28, :] = after(t)
        for g in range(groups):
            at = PAD + 8 * g
            ahead = Shifts(lambda t: face[1, t, at : at + 8, :], -1)
            behind = Shifts(ahead.tile, 1)
            for t in range(TILES):
                own = ahead.tile(t)
                total = face[1, t, at - 1 : at + 7, :] + face[1, t, at + 1 : at + 9, :]
                total = total + ahead.at(t) + behind.at(t)
                rows = slice(8 * g, 8 * g + 8)
                coef[1 + 3 * direction, t, rows, :] = VISCOSITY * own
                coef[2 + 3 * direction, t, rows, :] = own - VISCOSITY * own * total


def ocean_part(
    inbox, base, slabs, motion, ocean, floor, wide, first, coef, height, flow, side, row_left
):
    part, ocean_at, _, more_at = offsets(slabs)
    low = iota((8, LANES), 0) < 4
    groups = 4 if wide else 3

    def place(target, t, own, near, top, far):
        target[t, PAD - 4 : PAD + 4, :] = top
        target[t, PAD + 4 : PAD + 20, :] = own
        if wide:
            near = jnp.where(low, near, far)
            target[t, PAD + 28 : PAD + 36, :] = far
        target[t, PAD + 20 : PAD + 28, :] = near

    if first or wide:
        for t in range(TILES):
            for f, target in ((1, flow.at[0, 0]), (0, height)):
                near, top = base.halves(more_at + part, f * TILES + t)
                far = inbox.right(more_at + 8 * (UNITS + f * TILES + t)) if wide else None
                place(target, t, floor[f, t, :, :], near, top, far)
        after = lambda t: base.halves(more_at + part, 2 * TILES + t)[0]
        coefficients(coef, flow.at[0], height, None if wide else after)
    spread_left, spread_last = upsampled([row_left, motion[2, 1, 0:1, :]])
    for t in range(TILES):
        for f in range(3):
            near, top = inbox.halves(ocean_at, f * TILES + t)
            far = inbox.right(more_at + 8 * (f * TILES + t)) if wide else None
            target = height if f == 0 else flow.at[0, f - 1]
            place(target, t, ocean[f, t, :, :], near, top, far)
        for g in range(groups):
            spread = spread_left if g < 2 else spread_last
            lift = UPLIFT_GAIN * coef[7, t, 8 * g : 8 * g + 8, :] * spread[t : t + 1]
            lift = jnp.where(low == (g % 2 == 1), lift, 0.0)
            at = PAD + 8 * g
            height[t, at : at + 8, :] = height[t, at : at + 8, :] + lift
    for step in range(NSUB):
        old, new = step % 2, (step + 1) % 2
        for g in range(groups):
            at, rows = PAD + 8 * g, slice(8 * g, 8 * g + 8)
            n_behind = Shifts(lambda t: flow[old, 1, t, at : at + 8, :], 1)
            for t in range(TILES):
                m, n = flow[old, 0, t, at : at + 8, :], n_behind.tile(t)
                west = n_behind.at(t)
                if not (first and step == 0):
                    side[t, rows, :] = west
                spill = (m - flow[old, 0, t, at - 1 : at + 7, :]) + (n - west)
                height[t, at : at + 8, :] = height[t, at : at + 8, :] - coef[0, t, rows, :] * spill
        if first and step == 0:
            for t in range(TILES):
                for g in range(groups):
                    at, rows = PAD + 8 * g, slice(8 * g, 8 * g + 8)
                    for d in range(2):
                        wet = jnp.where(coef[1 + 3 * d, t, rows, :] > 0.0, 1.0, 0.0)
                        flow[old, d, t, at : at + 8, :] = wet * flow[old, d, t, at : at + 8, :]
        for g in range(groups):
            at, rows = PAD + 8 * g, slice(8 * g, 8 * g + 8)
            h_ahead = Shifts(lambda t: height[t, at : at + 8, :], -1)
            ahead = [Shifts(lambda t, d=d: flow[old, d, t, at : at + 8, :], -1) for d in range(2)]
            m_behind = Shifts(ahead[0].tile, 1)
            n_behind = Shifts(ahead[1].tile, 1)
            for t in range(TILES):
                h = height[t, at : at + 8, :]
                sides = [height[t, at + 1 : at + 9, :], h_ahead.at(t)]
                for d in range(2):
                    q = flow[old, d, t, at : at + 8, :]
                    around = flow[old, d, t, at - 1 : at + 7, :] + flow[old, d, t, at + 1 : at + 9, :]
                    around = around + ahead[d].at(t)
                    if d == 0:
                        around = around + m_behind.at(t)
                    elif first and step == 0:
                        around = around + n_behind.at(t)
                    else:
                        around = around + side[t, rows, :]
                    c = 1 + 3 * d
                    slope = (coef[c + 2, t, rows, :] + h + sides[d]) * (sides[d] - h)
                    value = coef[c + 1, t, rows, :] * q + coef[c, t, rows, :] * (around - slope)
                    flow[new, d, t, at : at + 8, :] = value


def step_kernel(last, is_first, edge, *refs):
    parity, refs = refs[0], list(refs[1:])

    def take(count):
        taken = refs[:count]
        del refs[:count]
        return taken

    base_one, base_two = take(2)
    one, two = (base_one, base_two) if is_first else take(2)
    motion, stress, solid, ocean, floor = take(5)
    ready = not (is_first or last)
    if ready:
        (coef,) = take(1)
    if last:
        motion_out, stress_out, surface_out, momentum_out = take(4)
    else:
        motion_out, stress_out, ocean_out, send_one, send_two = take(5)
    if not ready:
        (coef,) = take(1)
    height, flow, side, speed = take(4)
    slabs = motion.shape[2] // 8
    part, _, extra_at, more_at = offsets(slabs)
    even = parity[0] == 0
    base = Receiver(even, base_one, base_two)
    inbox = Receiver(even, one, two)

    def extra_row(take):
        return jnp.concatenate([take(extra_at)[0:1], take(extra_at + 8)[0:1]], axis=1)

    row_left = extra_row(inbox.left)
    loaded = None if is_first else -LOAD_GAIN * extra_row(inbox.right)
    ocean_part(
        inbox, base, slabs, motion, ocean, floor, last, is_first, coef, height, flow, side, row_left
    )
    blocks = 3 if last else 2
    sums = [[] for _ in range(blocks)]
    rows = slice(PAD + 4, PAD + 20)
    for t in range(TILES):
        for b in range(blocks):
            at = 8 * b + 4
            wet = coef[7, t, at : at + 8, :]
            h = height[t, PAD + at : PAD + at + 8, :]
            sums[b].append(jnp.sum(wet * h, axis=0, keepdims=True))
        if last:
            if t < TILES - 1:
                lanes = slice(LANES * t, LANES * t + LANES)
                surface_out[:, lanes] = height[t, rows, :]
                for d in range(2):
                    momentum_out[d, :, lanes] = flow[NSUB % 2, d, t, rows, :]
        else:
            ocean_out[0, t] = height[t, rows, :]
            for d in range(2):
                ocean_out[1 + d, t] = flow[NSUB % 2, d, t, rows, :]
    means = block_means(sums)

    def old(f, row):
        def get(k):
            value = stress[f, row, 8 * k : 8 * k + 8, :]
            if (f, row, k) == (2, 1, 0) and loaded is not None:
                value = jnp.where(iota(value.shape, 0) == 0, loaded, value)
            return value

        return get

    def new(f, row):
        return lambda k: speed[f, row, 8 * k : 8 * k + 8, :]

    for k in range(slabs):
        z = slice(8 * k, 8 * k + 8)
        xx = [stress[0, 0, z, :], stress[0, 1, z, :], inbox.solid(1, 2 * part, k, slabs)]
        xy = [inbox.solid(-1, part, k, slabs), stress[3, 0, z, :], stress[3, 1, z, :]]
        xz = [inbox.solid(-1, 2 * part, k, slabs), stress[4, 0, z, :], stress[4, 1, z, :]]
        rate_left = SOLID_STEP * base.solid(-1, more_at, k, slabs)
        rate_right = SOLID_STEP * base.solid(1, more_at, k, slabs)
        speed[0, 2, z, :] = inbox.solid(-1, 0, k, slabs) + rate_left * xx[0]
        speed[1, 2, z, :] = inbox.solid(1, 0, k, slabs) - rate_right * xy[2]
        speed[2, 2, z, :] = inbox.solid(1, part, k, slabs) - rate_right * xz[2]
        rates = [SOLID_STEP * solid[0, row, z, :] for row in range(2)]
        whole_x = (xx[1] - xx[0]) + (xy[1] - prev_lane(xy[1])) + (xz[1] - below(old(4, 0), k))
        yy, zz, yz = stress[1, 1, z, :], old(2, 1), stress[5, 1, z, :]
        whole_y = (xy[2] - xy[1]) + (next_lane(yy) - yy) + (yz - below(old(5, 1), k))
        whole_z = (xz[2] - xz[1]) + (yz - prev_lane(yz)) + (above(zz, k, slabs) - zz(k))
        forces = {
            (0, 0): whole_x, (0, 1): xx[2],
            (1, 0): -xy[0], (1, 1): whole_y,
            (2, 0): -xz[0], (2, 1): whole_z,
        }
        for (f, row), force in forces.items():
            value = motion[f, row, z, :] + rates[row] * force
            speed[f, row, z, :] = value
            motion_out[f, row, z, :] = value[:, :LANES] if last else value
    width = LANES if last else 2 * LANES
    for k in range(slabs):
        z = slice(8 * k, 8 * k + 8)
        x_of = [speed[0, 2, z, :], speed[0, 0, z, :], speed[0, 1, z, :]]
        y_of = [speed[1, 0, z, :], speed[1, 1, z, :], speed[1, 2, z, :]]
        z_of = [speed[2, 0, z, :], speed[2, 1, z, :], speed[2, 2, z, :]]
        for row in range(2):
            vx, vy, vz = x_of[row + 1], y_of[row], z_of[row]
            strain_x = vx - x_of[row]
            strain_y = vy - prev_lane(vy)
            strain_z = vz - below(new(2, row), k)
            shear = SOLID_STEP * solid[2, row, z, :]
            lame = SOLID_STEP * solid[1, row, z, :]
            common = lame * (strain_x + strain_y + strain_z)
            twice = shear + shear
            rates = [common + twice * strain for strain in (strain_x, strain_y, strain_z)]
            rates.append(shear * ((next_lane(vx) - vx) + (y_of[row + 1] - vy)))
            rates.append(shear * ((above(new(0, row), k, slabs) - vx) + (z_of[row + 1] - vz)))
            rates.append(shear * ((above(new(1, row), k, slabs) - vy) + (next_lane(vz) - vz)))
            for f in range(6):
                value = stress[f, row, z, :] + rates[f]
                stress_out[f, row, z, :] = value[:, :width]
    stress_out[2, 0, 0:1, :] = -LOAD_GAIN * means[1][:, :width]
    if last:
        stress_out[2, 1, 0:1, :] = -LOAD_GAIN * means[2][:, :width]
        return
    out = Sender(even, send_one, send_two)
    next_kind = "last" if edge else "usual"
    finish(out, slabs, motion_out, stress_out, solid, ocean_out, floor, means[0], next_kind)


def swap(size, start):
    pairs = []
    for i in range(start, size - 1, 2):
        pairs += [(i, i + 1), (i + 1, i)]
    return pairs


def exchanged(first, second, axis):
    size = lax.axis_size(axis)
    return (
        lax.ppermute(first, axis, swap(size, 0)),
        lax.ppermute(second, axis, swap(size, 1)),
    )


def body(motion, stress, buoyancy, lame_first, lame_shear, surface, momentum, bathymetry, wet_mask):
    depth_cells = motion.shape[2]
    slabs = depth_cells // 8
    f32 = jnp.float32

    def array(*shape):
        return jax.ShapeDtypeStruct(shape, f32)

    def call(kernel, outs, args, scratch=(), grant=VMEM_LIMIT):
        specs = [pl.BlockSpec(memory_space=pltpu.SMEM)]
        specs += [pl.BlockSpec(memory_space=pltpu.VMEM)] * (len(args) - 1)
        return pl.pallas_call(
            kernel,
            out_shape=outs,
            in_specs=specs,
            out_specs=tuple(pl.BlockSpec(memory_space=pltpu.VMEM) for _ in outs),
            scratch_shapes=list(scratch),
            compiler_params=pltpu.CompilerParams(vmem_limit_bytes=grant),
            interpret=INTERPRET,
        )(*args)

    parity = jnp.stack([lax.axis_index("gx") % 2, lax.axis_index("gy") % 2]).astype(jnp.int32)
    own = (
        motion, stress, buoyancy, lame_first, lame_shear, surface, momentum, bathymetry, wet_mask,
    )
    state = (array(3, 2, depth_cells, 256), array(6, 2, depth_cells, 256))
    wide = (
        *state,
        array(3, 2, depth_cells, 256),
        array(3, TILES, 16, LANES),
        array(2, TILES, 16, LANES),
    )
    packed = (array(pack_y_rows(slabs), LANES),) * 2
    received = exchanged(*call(pack_y_kernel, packed, (parity, *own), grant=LOADER_LIMIT), "gy")
    packed = (array(payload_rows(slabs, "first"), LANES),) * 2
    motion, stress, solid, ocean, floor, *send = call(
        start_kernel, (*wide, *packed), (parity, *own, *received)
    )
    base = coef = None
    for step in range(STEPS):
        received = exchanged(*send, "gx")
        first, last, edge = step == 0, step == STEPS - 1, step == STEPS - 2
        height = 32 if last else 24
        table = (8, TILES, height, LANES)
        padded = height + 2 * PAD
        scratch = [
            pltpu.VMEM((TILES, padded, LANES), f32),
            pltpu.VMEM((2, 2, TILES, padded, LANES), f32),
            pltpu.VMEM((TILES, height, LANES), f32),
            pltpu.VMEM((3, 3, depth_cells, 256), f32),
        ]
        rows = payload_rows(slabs, "last" if edge else "usual")
        outs = (*state, array(3, TILES, 16, LANES), array(rows, LANES), array(rows, LANES))
        fixed = (motion, stress, solid, ocean, floor)
        if first:
            base = received
            inputs = (parity, *base, *fixed)
            outs = (*outs, array(*table))
        elif last:
            inputs = (parity, *base, *received, *fixed)
            scratch = [pltpu.VMEM(table, f32), *scratch]
            outs = (
                array(3, 2, depth_cells, LANES),
                array(6, 2, depth_cells, LANES),
                array(16, 8 * LANES),
                array(2, 16, 8 * LANES),
            )
        else:
            inputs = (parity, *base, *received, *fixed, coef)
        kernel = functools.partial(step_kernel, last, first, edge)
        results = call(kernel, outs, inputs, scratch)
        if first:
            coef = results[-1]
        if not last:
            motion, stress, ocean, *send = results[:5]
    return results


def solution(mesh):
    return jax.shard_map(
        body,
        mesh=mesh,
        in_specs=(
            P(None, "gx", None, "gy"),
            P(None, "gx", None, "gy"),
            P("gx", None, "gy"),
            P("gx", None, "gy"),
            P("gx", None, "gy"),
            P("gx", "gy"),
            P(None, "gx", "gy"),
            P("gx", "gy"),
            P("gx", "gy"),
        ),
        out_specs=(
            P(None, "gx", None, "gy"),
            P(None, "gx", None, "gy"),
            P("gx", "gy"),
            P(None, "gx", "gy"),
        ),
        check_vma=False,
    )
```

```python
import functools

import jax
import jax.numpy as jnp
from jax import lax
from jax.experimental import pallas as pl
from jax.experimental.pallas import tpu as pltpu
from jax.sharding import PartitionSpec as P


STEPS = 4
NSUB = 4
SOLID_STEP = 0.2
WAVE_STEP = 0.1
VISCOSITY = 0.05
UPLIFT_GAIN = 0.25
LOAD_GAIN = 8.0

INTERPRET = False
VMEM_LIMIT = 20 << 20
LOADER_LIMIT = 62_000_000
LANES = 128
TILES = 9
UNITS = 3 * TILES
FLOOR_UNITS = 2 * TILES


def iota(shape, dim):
    return lax.broadcasted_iota(jnp.int32, shape, dim)


def roll(value, shift, axis):
    shift = shift % value.shape[axis]
    return value if shift == 0 else pltpu.roll(value, shift, axis)


def prev_lane(value):
    return roll(value, 1, 1)


def next_lane(value):
    return roll(value, -1, 1)


def below(get, k):
    current = roll(get(k), 1, 0)
    other = roll(get(k - 1), 1, 0) if k > 0 else jnp.zeros_like(current)
    return jnp.where(iota(current.shape, 0) == 0, other, current)


def above(get, k, slabs):
    current = roll(get(k), -1, 0)
    other = roll(get(k + 1), -1, 0) if k < slabs - 1 else jnp.zeros_like(current)
    return jnp.where(iota(current.shape, 0) == 7, other, current)


def expander():
    shape = (LANES, LANES)
    return jnp.where(iota(shape, 0) == iota(shape, 1) >> 3, 1.0, 0.0)


def reducer():
    shape = (LANES, LANES)
    return jnp.where(iota(shape, 0) >> 3 == iota(shape, 1), 1.0 / 64.0, 0.0)


def exact_dot(left, right):
    return jnp.dot(
        left, right, precision=lax.Precision.HIGHEST, preferred_element_type=jnp.float32
    )


def upsampled(rows):
    lane, line = iota((8, LANES), 1), iota((8, LANES), 0)
    stack = []
    for row in rows:
        own = jnp.broadcast_to(row[:, :LANES], (8, LANES))
        halo = jnp.broadcast_to(row[:, LANES:], (8, LANES))
        tiles = own
        for t in range(1, 8):
            tiles = jnp.where(line == t, roll(own, -16 * t, 1), tiles)
        stack += [tiles, jnp.where(lane < 4, halo, roll(halo, 16, 1))]
    spread = exact_dot(jnp.concatenate(stack, axis=0), expander())
    return [spread[16 * i : 16 * i + 16] for i in range(len(rows))]


def block_means(sums):
    lane, line = iota((8, LANES), 1), iota((8, LANES), 0)
    stack = []
    for tiles in sums:
        wide = [jnp.broadcast_to(tile, (8, LANES)) for tile in tiles]
        own = wide[0]
        for t in range(1, 8):
            own = jnp.where(line == t, wide[t], own)
        stack += [own, wide[8]]
    mean = exact_dot(jnp.concatenate(stack, axis=0), reducer())
    rows = []
    for i in range(len(sums)):
        tiles, last = mean[16 * i : 16 * i + 8], mean[16 * i + 8 : 16 * i + 16]
        own = jnp.zeros((8, LANES), jnp.float32)
        for t in range(8):
            own = jnp.where((line == t) & (lane >> 4 == t), roll(tiles, 16 * t, 1), own)
        own = jnp.sum(own, axis=0, keepdims=True)
        halo = jnp.where(lane < 4, last, jnp.where(lane >= 124, roll(last, 112, 1), 0.0))
        rows.append(jnp.concatenate([own, halo[0:1]], axis=1))
    return rows


class Sender:
    def __init__(self, even, first_ref, second_ref):
        self.even, self.first, self.second = even, first_ref, second_ref

    def put(self, at, right, left):
        end = at + right.shape[0]
        self.first[at:end, :] = jnp.where(self.even, right, left)
        self.second[at:end, :] = jnp.where(self.even, left, right)

    def put_solid(self, at, slabs, right, left):
        lane = iota((8, LANES), 1)
        tails = [jnp.zeros((8, LANES), jnp.float32) for _ in range(2)]
        for k in range(slabs):
            here = (lane >= 8 * k) & (lane < 8 * k + 8)
            values = (right(k), left(k))
            for i, value in enumerate(values):
                tails[i] = jnp.where(here, roll(value[:, LANES:], 4 + 8 * k, 1), tails[i])
            self.put(at + 8 * k, values[0][:, :LANES], values[1][:, :LANES])
        self.put(at + 8 * slabs, *tails)

    def put_tail(self, at, slabs, right, left):
        lane = iota((8, LANES), 1)
        tails = [jnp.zeros((8, LANES), jnp.float32) for _ in range(2)]
        for k in range(slabs):
            here = (lane >= 8 * k) & (lane < 8 * k + 8)
            for i, value in enumerate((right(k), left(k))):
                tails[i] = jnp.where(here, roll(value[:, LANES:], 4 + 8 * k, 1), tails[i])
        self.put(at, *tails)

    def put_halves(self, at, units):
        low = iota((8, LANES), 0) < 4
        for i in range(0, len(units), 2):
            (lower, upper), (lower2, upper2) = units[i], units[min(i + 1, len(units) - 1)]
            right = jnp.where(low, roll(upper, 4, 0), upper2)
            left = jnp.where(low, lower, roll(lower2, 4, 0))
            self.put(at + 4 * i, right, left)


class Receiver:
    def __init__(self, even, first_ref, second_ref):
        self.even, self.first, self.second = even, first_ref, second_ref

    def right(self, at):
        return jnp.where(self.even, self.first[at : at + 8, :], self.second[at : at + 8, :])

    def left(self, at):
        return jnp.where(self.even, self.second[at : at + 8, :], self.first[at : at + 8, :])

    def halves(self, at, unit):
        at = at + 8 * (unit // 2)
        near, top = self.right(at), self.left(at)
        near = roll(near, 4, 0) if unit % 2 else near
        top = top if unit % 2 else roll(top, 4, 0)
        return near, top

    def solid(self, side, at, k, slabs):
        take = self.right if side > 0 else self.left
        tail = roll(take(at + 8 * slabs), -(4 + 8 * k), 1)
        return jnp.concatenate([take(at + 8 * k), tail], axis=1)


def offsets(slabs):
    part = 8 * slabs + 8
    ocean = 3 * part
    extra = ocean + 8 * ((UNITS + 1) // 2)
    more = extra + 16
    return part, ocean, extra, more


def payload_rows(slabs, kind):
    _, _, _, more = offsets(slabs)
    return {
        "first": more + 24,
        "usual": more,
        "last": more + 8 * (UNITS + FLOOR_UNITS),
    }[kind]


def floor_units(depth, wet):
    face = wet * roll(wet, -1, 0)
    return [(value[0:8], value[8:16]) for value in (depth, wet, face)]


def static_rows(slabs):
    return 8 * slabs + 8 * 3 * (TILES - 1) // 2


def finish(out, slabs, motion, stress, buoyancy, ocean, floor, mean_row, kind):
    part, ocean_at, extra_at, more_at = offsets(slabs)
    low = iota((8, LANES), 0) < 4

    def get(ref, field, row):
        return lambda k: ref[field, row, 8 * k : 8 * k + 8, :]

    def rate(row, k):
        return SOLID_STEP * buoyancy[0, row, 8 * k : 8 * k + 8, :]

    def sum_x(k):
        xx, xy, xz = (get(stress, f, 1) for f in (0, 3, 4))
        mid = xy(k)
        force = (mid - prev_lane(mid)) + (xz(k) - below(xz, k)) - xx(k)
        return get(motion, 0, 1)(k) + rate(1, k) * force

    def sum_y(k):
        xy, yy, yz = (get(stress, f, 0) for f in (3, 1, 5))
        mid = yy(k)
        force = xy(k) + (next_lane(mid) - mid) + (yz(k) - below(yz, k))
        return get(motion, 1, 0)(k) + rate(0, k) * force

    def sum_z(k):
        xz, yz, zz = (get(stress, f, 0) for f in (4, 5, 2))
        mid = yz(k)
        force = xz(k) + (mid - prev_lane(mid)) + (above(zz, k, slabs) - zz(k))
        return get(motion, 2, 0)(k) + rate(0, k) * force

    def kept(compute, field, row):
        def get_and_keep(k):
            value = compute(k)
            motion[field, row, 8 * k : 8 * k + 8, :] = value
            return value

        return get_and_keep

    (spread,) = upsampled([motion[2, 0, 0:1, :]])
    out.put_solid(0, slabs, kept(sum_x, 0, 1), kept(sum_y, 1, 0))
    out.put_solid(part, slabs, get(stress, 3, 1), kept(sum_z, 2, 0))
    out.put_solid(2 * part, slabs, get(stress, 4, 1), get(stress, 0, 0))
    for t in range(TILES):
        ocean[0, t, 8:16, :] = (
            ocean[0, t, 8:16, :] + UPLIFT_GAIN * floor[1, t, 8:16, :] * spread[t : t + 1]
        )

    def units(ref, fields):
        pairs = [(f, t) for f in range(fields) for t in range(TILES)]
        return [(ref[f, t, 0:8, :], ref[f, t, 8:16, :]) for f, t in pairs]

    out.put_halves(ocean_at, units(ocean, 3))
    top = motion[2, 1, 0:8, :]
    mean_row = jnp.zeros((8, 256), jnp.float32) if mean_row is None else mean_row
    mean_row = jnp.broadcast_to(mean_row, (8, 256))
    for i in range(2):
        lanes = slice(LANES * i, LANES * i + LANES)
        out.put(extra_at + 8 * i, top[:, lanes], mean_row[:, lanes])
    if kind == "first":
        out.put_tail(more_at, slabs, get(buoyancy, 0, 1), get(buoyancy, 0, 0))
        last = TILES - 1
        out.put_halves(more_at + 8, floor_units(floor[0, last, :, :], floor[1, last, :, :]))
    if kind == "last":
        for i, (lower, upper) in enumerate(units(ocean, 3) + units(floor, 2)):
            value = jnp.where(low, upper, lower)
            out.put(more_at + 8 * i, value, value)


def pack_y_kernel(
    motion, stress, buoyancy, first, shear, surface, momentum, depth, wet, one, two,
    static_one, static_two,
):
    even = lax.rem(lax.axis_index("gy"), 2) == 0
    out = Sender(even, one, two)
    slabs = motion.shape[2] // 8
    lane = iota((8, LANES), 1)
    fields = [(motion, f) for f in range(3)] + [(stress, f) for f in range(6)]
    fields += [(buoyancy, None), (first, None), (shear, None)]
    count, at = 0, 0
    right = left = jnp.zeros((8, LANES), jnp.float32)
    for ref, f in fields:
        for row in range(2):
            for k in range(slabs):
                z = slice(8 * k, 8 * k + 8)
                value = ref[row, z, :] if f is None else ref[f, row, z, :]
                here = lane >> 2 == count
                right = jnp.where(here, roll(value, 4 * count + 4, 1), right)
                left = jnp.where(here, roll(value, 4 * count, 1), left)
                count += 1
                if count == 32:
                    out.put(at, right, left)
                    count, at = 0, at + 8
    if count:
        out.put(at, right, left)
        count, at = 0, at + 8
    width = surface.shape[1]
    for ref, f in ((surface, None), (momentum, 0), (momentum, 1), (depth, None), (wet, None)):
        for group in range(2):
            rows = slice(8 * group, 8 * group + 8)
            ends = []
            for lanes in (slice(0, LANES), slice(width - LANES, width)):
                value = ref[rows, lanes] if f is None else ref[f, rows, lanes]
                ends.append(value.astype(jnp.float32))
            here = lane >> 5 == count
            right = jnp.where(here, roll(ends[1], 32 * count + 32, 1), right)
            left = jnp.where(here, roll(ends[0], 32 * count, 1), left)
            count += 1
            if count == 4:
                out.put(at, right, left)
                count, at = 0, at + 8
    if count:
        out.put(at, right, left)
    out = Sender(lax.rem(lax.axis_index("gx"), 2) == 0, static_one, static_two)
    for k in range(slabs):
        out.put(8 * k, buoyancy[1, 8 * k : 8 * k + 8, :], buoyancy[0, 8 * k : 8 * k + 8, :])
    units = []
    for t in range(TILES - 1):
        lanes = slice(LANES * t, LANES * t + LANES)
        units += floor_units(depth[:, lanes], wet[:, lanes].astype(jnp.float32))
    out.put_halves(8 * slabs, units)


def pack_y_rows(slabs):
    return 8 * (-(-24 * slabs // 32) + 3)


def start_kernel(
    motion, stress, buoyancy, first, shear, surface, momentum, depth, wet, one, two,
    motion_out, stress_out, solid_out, ocean_out, floor_out, send_one, send_two,
):
    inbox = Receiver(lax.rem(lax.axis_index("gy"), 2) == 0, one, two)
    slabs = motion.shape[2] // 8
    lane = iota((8, LANES), 1)
    fields = [(motion, f, motion_out, f) for f in range(3)]
    fields += [(stress, f, stress_out, f) for f in range(6)]
    fields += [(ref, None, solid_out, f) for f, ref in enumerate((buoyancy, first, shear))]
    count, at = 0, 0
    for ref, f, target, g in fields:
        for row in range(2):
            for k in range(slabs):
                z = slice(8 * k, 8 * k + 8)
                value = ref[row, z, :] if f is None else ref[f, row, z, :]
                if count == 0:
                    packed = inbox.right(at), inbox.left(at)
                after = roll(packed[0], -4 * count, 1)
                before = roll(packed[1], 124 - 4 * count, 1)
                halo = jnp.where(lane < 4, after, jnp.where(lane >= 124, before, 0.0))
                target[g, row, z, 0:LANES] = value
                target[g, row, z, LANES : 2 * LANES] = halo
                count += 1
                if count == 32:
                    count, at = 0, at + 8
    if count:
        count, at = 0, at + 8
    targets = ((surface, None), (momentum, 0), (momentum, 1), (depth, None), (wet, None))
    for i, (ref, f) in enumerate(targets):
        for group in range(2):
            rows = slice(8 * group, 8 * group + 8)
            if count == 0:
                packed = inbox.right(at), inbox.left(at)
            after = roll(packed[0], -32 * count, 1)
            before = roll(packed[1], 96 - 32 * count, 1)
            halo = jnp.where(lane < 32, after, jnp.where(lane >= 96, before, 0.0))
            for t in range(TILES):
                if t == TILES - 1:
                    value = halo
                else:
                    lanes = slice(LANES * t, LANES * t + LANES)
                    value = ref[rows, lanes] if f is None else ref[f, rows, lanes]
                    value = value.astype(jnp.float32)
                if i < 3:
                    ocean_out[i, t, rows, :] = value
                else:
                    floor_out[i - 3, t, rows, :] = value
            count += 1
            if count == 4:
                count, at = 0, at + 8
    out = Sender(lax.rem(lax.axis_index("gx"), 2) == 0, send_one, send_two)
    finish(out, slabs, motion_out, stress_out, solid_out, ocean_out, floor_out, None, "first")


PAD = 8


class Shifts:
    def __init__(self, tile, by):
        self.tile, self.by, self.rolled = tile, by, {}

    def rotated(self, t):
        if t not in self.rolled:
            self.rolled[t] = roll(self.tile(t), self.by, 1)
        return self.rolled[t]

    def at(self, t):
        lane = iota((8, LANES), 1)
        other, mine = self.rotated((t - self.by) % TILES), self.rotated(t)
        return jnp.where(lane == (0 if self.by > 0 else LANES - 1), other, mine)


def coefficients(coef, face, depth, after):
    groups = coef.shape[2] // 8
    for t in range(TILES):
        for g in range(groups):
            at = PAD + 8 * g
            wet = face[0, t, at : at + 8, :]
            coef[7, t, 8 * g : 8 * g + 8, :] = wet
            coef[0, t, 8 * g : 8 * g + 8, :] = WAVE_STEP * wet
    for direction in range(2):
        for g in range(groups):
            at = PAD + 8 * g
            wets = Shifts(lambda t: coef[7, t, 8 * g : 8 * g + 8, :], -1)
            depths = Shifts(lambda t: depth[t, at : at + 8, :], -1)
            for t in range(TILES):
                wet = wets.tile(t)
                here = depths.tile(t)
                if direction == 0:
                    beside = face[0, t, at + 1 : at + 9, :]
                    deep = depth[t, at + 1 : at + 9, :]
                else:
                    beside, deep = wets.at(t), depths.at(t)
                face[1, t, at : at + 8, :] = wet * beside
                coef[3 + 3 * direction, t, 8 * g : 8 * g + 8, :] = here + deep
        if direction == 0 and after is not None:
            for t in range(TILES):
                face[1, t, PAD + 20 : PAD + 28, :] = after(t)
        for g in range(groups):
            at = PAD + 8 * g
            ahead = Shifts(lambda t: face[1, t, at : at + 8, :], -1)
            behind = Shifts(ahead.tile, 1)
            for t in range(TILES):
                own = ahead.tile(t)
                total = face[1, t, at - 1 : at + 7, :] + face[1, t, at + 1 : at + 9, :]
                total = total + ahead.at(t) + behind.at(t)
                rows = slice(8 * g, 8 * g + 8)
                coef[1 + 3 * direction, t, rows, :] = VISCOSITY * own
                coef[2 + 3 * direction, t, rows, :] = own - VISCOSITY * own * total


def ocean_part(
    inbox, bases, slabs, motion, ocean, floor, wide, first, coef, height, flow, side, row_left
):
    _, ocean_at, _, more_at = offsets(slabs)
    low = iota((8, LANES), 0) < 4
    groups = 4 if wide else 3

    def place(target, t, own, near, top, far):
        target[t, PAD - 4 : PAD + 4, :] = top
        target[t, PAD + 4 : PAD + 20, :] = own
        if wide:
            near = jnp.where(low, near, far)
            target[t, PAD + 28 : PAD + 36, :] = far
        target[t, PAD + 20 : PAD + 28, :] = near

    def floor_halves(f, t):
        if t < TILES - 1:
            return bases[0].halves(8 * slabs, 3 * t + f)
        return bases[1].halves(more_at + 8, f)

    if first or wide:
        for t in range(TILES):
            for f, target in ((1, flow.at[0, 0]), (0, height)):
                near, top = floor_halves(f, t)
                far = inbox.right(more_at + 8 * (UNITS + f * TILES + t)) if wide else None
                place(target, t, floor[f, t, :, :], near, top, far)
        after = lambda t: floor_halves(2, t)[0]
        coefficients(coef, flow.at[0], height, None if wide else after)
    spread_left, spread_last = upsampled([row_left, motion[2, 1, 0:1, :]])
    for t in range(TILES):
        for f in range(3):
            near, top = inbox.halves(ocean_at, f * TILES + t)
            far = inbox.right(more_at + 8 * (f * TILES + t)) if wide else None
            target = height if f == 0 else flow.at[0, f - 1]
            place(target, t, ocean[f, t, :, :], near, top, far)
        for g in range(groups):
            spread = spread_left if g < 2 else spread_last
            lift = UPLIFT_GAIN * coef[7, t, 8 * g : 8 * g + 8, :] * spread[t : t + 1]
            lift = jnp.where(low == (g % 2 == 1), lift, 0.0)
            at = PAD + 8 * g
            height[t, at : at + 8, :] = height[t, at : at + 8, :] + lift
    for step in range(NSUB):
        old, new = step % 2, (step + 1) % 2
        for g in range(groups):
            at, rows = PAD + 8 * g, slice(8 * g, 8 * g + 8)
            n_behind = Shifts(lambda t: flow[old, 1, t, at : at + 8, :], 1)
            for t in range(TILES):
                m, n = flow[old, 0, t, at : at + 8, :], n_behind.tile(t)
                west = n_behind.at(t)
                if not (first and step == 0):
                    side[t, rows, :] = west
                spill = (m - flow[old, 0, t, at - 1 : at + 7, :]) + (n - west)
                height[t, at : at + 8, :] = height[t, at : at + 8, :] - coef[0, t, rows, :] * spill
        if first and step == 0:
            for t in range(TILES):
                for g in range(groups):
                    at, rows = PAD + 8 * g, slice(8 * g, 8 * g + 8)
                    for d in range(2):
                        wet = jnp.where(coef[1 + 3 * d, t, rows, :] > 0.0, 1.0, 0.0)
                        flow[old, d, t, at : at + 8, :] = wet * flow[old, d, t, at : at + 8, :]
        for g in range(groups):
            at, rows = PAD + 8 * g, slice(8 * g, 8 * g + 8)
            h_ahead = Shifts(lambda t: height[t, at : at + 8, :], -1)
            ahead = [Shifts(lambda t, d=d: flow[old, d, t, at : at + 8, :], -1) for d in range(2)]
            m_behind = Shifts(ahead[0].tile, 1)
            n_behind = Shifts(ahead[1].tile, 1)
            for t in range(TILES):
                h = height[t, at : at + 8, :]
                sides = [height[t, at + 1 : at + 9, :], h_ahead.at(t)]
                for d in range(2):
                    q = flow[old, d, t, at : at + 8, :]
                    around = flow[old, d, t, at - 1 : at + 7, :] + flow[old, d, t, at + 1 : at + 9, :]
                    around = around + ahead[d].at(t)
                    if d == 0:
                        around = around + m_behind.at(t)
                    elif first and step == 0:
                        around = around + n_behind.at(t)
                    else:
                        around = around + side[t, rows, :]
                    c = 1 + 3 * d
                    slope = (coef[c + 2, t, rows, :] + h + sides[d]) * (sides[d] - h)
                    value = coef[c + 1, t, rows, :] * q + coef[c, t, rows, :] * (around - slope)
                    flow[new, d, t, at : at + 8, :] = value


def step_kernel(last, is_first, edge, *refs):
    refs = list(refs)

    def take(count):
        taken = refs[:count]
        del refs[:count]
        return taken

    static_one, static_two, base_one, base_two = take(4)
    one, two = (base_one, base_two) if is_first else take(2)
    motion, stress, solid, ocean, floor = take(5)
    ready = not (is_first or last)
    if ready:
        (coef,) = take(1)
    if last:
        motion_out, stress_out, surface_out, momentum_out = take(4)
    else:
        motion_out, stress_out, ocean_out, send_one, send_two = take(5)
    if not ready:
        (coef,) = take(1)
    height, flow, side, speed = take(4)
    slabs = motion.shape[2] // 8
    part, _, extra_at, more_at = offsets(slabs)
    even = lax.rem(lax.axis_index("gx"), 2) == 0
    bases = [Receiver(even, static_one, static_two), Receiver(even, base_one, base_two)]
    inbox = Receiver(even, one, two)

    def extra_row(take):
        return jnp.concatenate([take(extra_at)[0:1], take(extra_at + 8)[0:1]], axis=1)

    row_left = extra_row(inbox.left)
    loaded = None if is_first else -LOAD_GAIN * extra_row(inbox.right)
    ocean_part(
        inbox, bases, slabs, motion, ocean, floor, last, is_first, coef, height, flow, side, row_left
    )
    blocks = 3 if last else 2
    sums = [[] for _ in range(blocks)]
    rows = slice(PAD + 4, PAD + 20)
    for t in range(TILES):
        for b in range(blocks):
            at = 8 * b + 4
            wet = coef[7, t, at : at + 8, :]
            h = height[t, PAD + at : PAD + at + 8, :]
            sums[b].append(jnp.sum(wet * h, axis=0, keepdims=True))
        if last:
            if t < TILES - 1:
                lanes = slice(LANES * t, LANES * t + LANES)
                surface_out[:, lanes] = height[t, rows, :]
                for d in range(2):
                    momentum_out[d, :, lanes] = flow[NSUB % 2, d, t, rows, :]
        else:
            ocean_out[0, t] = height[t, rows, :]
            for d in range(2):
                ocean_out[1 + d, t] = flow[NSUB % 2, d, t, rows, :]
    means = block_means(sums)

    def old(f, row):
        def get(k):
            value = stress[f, row, 8 * k : 8 * k + 8, :]
            if (f, row, k) == (2, 1, 0) and loaded is not None:
                value = jnp.where(iota(value.shape, 0) == 0, loaded, value)
            return value

        return get

    def new(f, row):
        return lambda k: speed[f, row, 8 * k : 8 * k + 8, :]

    for k in range(slabs):
        z = slice(8 * k, 8 * k + 8)
        xx = [stress[0, 0, z, :], stress[0, 1, z, :], inbox.solid(1, 2 * part, k, slabs)]
        xy = [inbox.solid(-1, part, k, slabs), stress[3, 0, z, :], stress[3, 1, z, :]]
        xz = [inbox.solid(-1, 2 * part, k, slabs), stress[4, 0, z, :], stress[4, 1, z, :]]
        tail_left = roll(bases[1].left(more_at), -(4 + 8 * k), 1)
        tail_right = roll(bases[1].right(more_at), -(4 + 8 * k), 1)
        rate_left = SOLID_STEP * jnp.concatenate([bases[0].left(8 * k), tail_left], axis=1)
        rate_right = SOLID_STEP * jnp.concatenate([bases[0].right(8 * k), tail_right], axis=1)
        speed[0, 2, z, :] = inbox.solid(-1, 0, k, slabs) + rate_left * xx[0]
        speed[1, 2, z, :] = inbox.solid(1, 0, k, slabs) - rate_right * xy[2]
        speed[2, 2, z, :] = inbox.solid(1, part, k, slabs) - rate_right * xz[2]
        rates = [SOLID_STEP * solid[0, row, z, :] for row in range(2)]
        whole_x = (xx[1] - xx[0]) + (xy[1] - prev_lane(xy[1])) + (xz[1] - below(old(4, 0), k))
        yy, zz, yz = stress[1, 1, z, :], old(2, 1), stress[5, 1, z, :]
        whole_y = (xy[2] - xy[1]) + (next_lane(yy) - yy) + (yz - below(old(5, 1), k))
        whole_z = (xz[2] - xz[1]) + (yz - prev_lane(yz)) + (above(zz, k, slabs) - zz(k))
        forces = {
            (0, 0): whole_x, (0, 1): xx[2],
            (1, 0): -xy[0], (1, 1): whole_y,
            (2, 0): -xz[0], (2, 1): whole_z,
        }
        for (f, row), force in forces.items():
            value = motion[f, row, z, :] + rates[row] * force
            speed[f, row, z, :] = value
            motion_out[f, row, z, :] = value[:, :LANES] if last else value
    width = LANES if last else 2 * LANES
    for k in range(slabs):
        z = slice(8 * k, 8 * k + 8)
        x_of = [speed[0, 2, z, :], speed[0, 0, z, :], speed[0, 1, z, :]]
        y_of = [speed[1, 0, z, :], speed[1, 1, z, :], speed[1, 2, z, :]]
        z_of = [speed[2, 0, z, :], speed[2, 1, z, :], speed[2, 2, z, :]]
        for row in range(2):
            vx, vy, vz = x_of[row + 1], y_of[row], z_of[row]
            strain_x = vx - x_of[row]
            strain_y = vy - prev_lane(vy)
            strain_z = vz - below(new(2, row), k)
            shear = SOLID_STEP * solid[2, row, z, :]
            lame = SOLID_STEP * solid[1, row, z, :]
            common = lame * (strain_x + strain_y + strain_z)
            twice = shear + shear
            rates = [common + twice * strain for strain in (strain_x, strain_y, strain_z)]
            rates.append(shear * ((next_lane(vx) - vx) + (y_of[row + 1] - vy)))
            rates.append(shear * ((above(new(0, row), k, slabs) - vx) + (z_of[row + 1] - vz)))
            rates.append(shear * ((above(new(1, row), k, slabs) - vy) + (next_lane(vz) - vz)))
            for f in range(6):
                value = stress[f, row, z, :] + rates[f]
                stress_out[f, row, z, :] = value[:, :width]
    stress_out[2, 0, 0:1, :] = -LOAD_GAIN * means[1][:, :width]
    if last:
        stress_out[2, 1, 0:1, :] = -LOAD_GAIN * means[2][:, :width]
        return
    out = Sender(even, send_one, send_two)
    next_kind = "last" if edge else "usual"
    finish(out, slabs, motion_out, stress_out, solid, ocean_out, floor, means[0], next_kind)


def swap(size, start):
    pairs = []
    for i in range(start, size - 1, 2):
        pairs += [(i, i + 1), (i + 1, i)]
    return pairs


def exchanged(first, second, axis):
    size = lax.axis_size(axis)
    return (
        lax.ppermute(first, axis, swap(size, 0)),
        lax.ppermute(second, axis, swap(size, 1)),
    )


def body(motion, stress, buoyancy, lame_first, lame_shear, surface, momentum, bathymetry, wet_mask):
    depth_cells = motion.shape[2]
    slabs = depth_cells // 8
    f32 = jnp.float32

    def array(*shape):
        return jax.ShapeDtypeStruct(shape, f32)

    def call(kernel, outs, args, scratch=(), grant=VMEM_LIMIT):
        specs = [pl.BlockSpec(memory_space=pltpu.VMEM)] * len(args)
        return pl.pallas_call(
            kernel,
            out_shape=outs,
            in_specs=specs,
            out_specs=tuple(pl.BlockSpec(memory_space=pltpu.VMEM) for _ in outs),
            scratch_shapes=list(scratch),
            compiler_params=pltpu.CompilerParams(vmem_limit_bytes=grant),
            interpret=INTERPRET,
        )(*args)

    own = (
        motion, stress, buoyancy, lame_first, lame_shear, surface, momentum, bathymetry, wet_mask,
    )
    state = (array(3, 2, depth_cells, 256), array(6, 2, depth_cells, 256))
    wide = (
        *state,
        array(3, 2, depth_cells, 256),
        array(3, TILES, 16, LANES),
        array(2, TILES, 16, LANES),
    )
    packed = (
        *(array(pack_y_rows(slabs), LANES),) * 2,
        *(array(static_rows(slabs), LANES),) * 2,
    )
    *send, static_one, static_two = call(pack_y_kernel, packed, own, grant=LOADER_LIMIT)
    received = exchanged(*send, "gy")
    static = exchanged(static_one, static_two, "gx")
    packed = (array(payload_rows(slabs, "first"), LANES),) * 2
    motion, stress, solid, ocean, floor, *send = call(
        start_kernel, (*wide, *packed), (*own, *received)
    )
    base = coef = None
    for step in range(STEPS):
        received = exchanged(*send, "gx")
        first, last, edge = step == 0, step == STEPS - 1, step == STEPS - 2
        height = 32 if last else 24
        table = (8, TILES, height, LANES)
        padded = height + 2 * PAD
        scratch = [
            pltpu.VMEM((TILES, padded, LANES), f32),
            pltpu.VMEM((2, 2, TILES, padded, LANES), f32),
            pltpu.VMEM((TILES, height, LANES), f32),
            pltpu.VMEM((3, 3, depth_cells, 256), f32),
        ]
        rows = payload_rows(slabs, "last" if edge else "usual")
        outs = (*state, array(3, TILES, 16, LANES), array(rows, LANES), array(rows, LANES))
        fixed = (motion, stress, solid, ocean, floor)
        if first:
            base = (*static, *received)
            inputs = (*base, *fixed)
            outs = (*outs, array(*table))
        elif last:
            inputs = (*base, *received, *fixed)
            scratch = [pltpu.VMEM(table, f32), *scratch]
            outs = (
                array(3, 2, depth_cells, LANES),
                array(6, 2, depth_cells, LANES),
                array(16, 8 * LANES),
                array(2, 16, 8 * LANES),
            )
        else:
            inputs = (*base, *received, *fixed, coef)
        kernel = functools.partial(step_kernel, last, first, edge)
        results = call(kernel, outs, inputs, scratch)
        if first:
            coef = results[-1]
        if not last:
            motion, stress, ocean, *send = results[:5]
    return results


def solution(mesh):
    return jax.shard_map(
        body,
        mesh=mesh,
        in_specs=(
            P(None, "gx", None, "gy"),
            P(None, "gx", None, "gy"),
            P("gx", None, "gy"),
            P("gx", None, "gy"),
            P("gx", None, "gy"),
            P("gx", "gy"),
            P(None, "gx", "gy"),
            P("gx", "gy"),
            P("gx", "gy"),
        ),
        out_specs=(
            P(None, "gx", None, "gy"),
            P(None, "gx", None, "gy"),
            P("gx", "gy"),
            P(None, "gx", "gy"),
        ),
        check_vma=False,
    )
```

```python
import functools

import jax
import jax.numpy as jnp
from jax import lax
from jax.experimental import pallas as pl
from jax.experimental.pallas import tpu as pltpu
from jax.sharding import PartitionSpec as P

STEPS = 4
NSUB = 4
SOLID_STEP = 0.2
WAVE_STEP = 0.1
VISCOSITY = 0.05
UPLIFT_GAIN = 0.25
LOAD_GAIN = 8.0

INTERPRET = False
VMEM_LIMIT = 20 << 20
LOADER_LIMIT = 62_000_000
LANES = 128
TILES = 9
UNITS = 3 * TILES
FLOOR_UNITS = 2 * TILES


def iota(shape, dim):
    return lax.broadcasted_iota(jnp.int32, shape, dim)


def roll(value, shift, axis):
    shift = shift % value.shape[axis]
    return value if shift == 0 else pltpu.roll(value, shift, axis)


def prev_lane(value):
    return roll(value, 1, 1)


def next_lane(value):
    return roll(value, -1, 1)


def below(get, k):
    current = roll(get(k), 1, 0)
    other = roll(get(k - 1), 1, 0) if k > 0 else jnp.zeros_like(current)
    return jnp.where(iota(current.shape, 0) == 0, other, current)


def above(get, k, slabs):
    current = roll(get(k), -1, 0)
    other = roll(get(k + 1), -1, 0) if k < slabs - 1 else jnp.zeros_like(current)
    return jnp.where(iota(current.shape, 0) == 7, other, current)


def expander():
    shape = (LANES, LANES)
    return jnp.where(iota(shape, 0) == iota(shape, 1) >> 3, 1.0, 0.0)


def reducer():
    shape = (LANES, LANES)
    return jnp.where(iota(shape, 0) >> 3 == iota(shape, 1), 1.0 / 64.0, 0.0)


def exact_dot(left, right):
    return jnp.dot(
        left, right, precision=lax.Precision.HIGHEST, preferred_element_type=jnp.float32
    )


def upsampled(rows):
    lane, line = iota((8, LANES), 1), iota((8, LANES), 0)
    stack = []
    for row in rows:
        own = jnp.broadcast_to(row[:, :LANES], (8, LANES))
        halo = jnp.broadcast_to(row[:, LANES:], (8, LANES))
        tiles = own
        for t in range(1, 8):
            tiles = jnp.where(line == t, roll(own, -16 * t, 1), tiles)
        stack += [tiles, jnp.where(lane < 4, halo, roll(halo, 16, 1))]
    spread = exact_dot(jnp.concatenate(stack, axis=0), expander())
    return [spread[16 * i : 16 * i + 16] for i in range(len(rows))]


def block_means(sums):
    lane, line = iota((8, LANES), 1), iota((8, LANES), 0)
    stack = []
    for tiles in sums:
        wide = [jnp.broadcast_to(tile, (8, LANES)) for tile in tiles]
        own = wide[0]
        for t in range(1, 8):
            own = jnp.where(line == t, wide[t], own)
        stack += [own, wide[8]]
    mean = exact_dot(jnp.concatenate(stack, axis=0), reducer())
    rows = []
    for i in range(len(sums)):
        tiles, last = mean[16 * i : 16 * i + 8], mean[16 * i + 8 : 16 * i + 16]
        own = jnp.zeros((8, LANES), jnp.float32)
        for t in range(8):
            own = jnp.where((line == t) & (lane >> 4 == t), roll(tiles, 16 * t, 1), own)
        own = jnp.sum(own, axis=0, keepdims=True)
        halo = jnp.where(lane < 4, last, jnp.where(lane >= 124, roll(last, 112, 1), 0.0))
        rows.append(jnp.concatenate([own, halo[0:1]], axis=1))
    return rows


class Sender:
    def __init__(self, even, first_ref, second_ref):
        self.even, self.first, self.second = even, first_ref, second_ref

    def put(self, at, right, left):
        end = at + right.shape[0]
        self.first[at:end, :] = jnp.where(self.even, right, left)
        self.second[at:end, :] = jnp.where(self.even, left, right)

    def put_solid(self, at, slabs, right, left):
        lane = iota((8, LANES), 1)
        tails = [jnp.zeros((8, LANES), jnp.float32) for _ in range(2)]
        for k in range(slabs):
            here = (lane >= 8 * k) & (lane < 8 * k + 8)
            values = (right(k), left(k))
            for i, value in enumerate(values):
                tails[i] = jnp.where(here, roll(value[:, LANES:], 4 + 8 * k, 1), tails[i])
            self.put(at + 8 * k, values[0][:, :LANES], values[1][:, :LANES])
        self.put(at + 8 * slabs, *tails)


    def put_halves(self, at, units):
        low = iota((8, LANES), 0) < 4
        for i in range(0, len(units), 2):
            (lower, upper), (lower2, upper2) = units[i], units[min(i + 1, len(units) - 1)]
            right = jnp.where(low, roll(upper, 4, 0), upper2)
            left = jnp.where(low, lower, roll(lower2, 4, 0))
            self.put(at + 4 * i, right, left)


class Receiver:
    def __init__(self, even, first_ref, second_ref):
        self.even, self.first, self.second = even, first_ref, second_ref

    def right(self, at):
        return jnp.where(self.even, self.first[at : at + 8, :], self.second[at : at + 8, :])

    def left(self, at):
        return jnp.where(self.even, self.second[at : at + 8, :], self.first[at : at + 8, :])

    def halves(self, at, unit):
        at = at + 8 * (unit // 2)
        near, top = self.right(at), self.left(at)
        near = roll(near, 4, 0) if unit % 2 else near
        top = top if unit % 2 else roll(top, 4, 0)
        return near, top

    def solid(self, side, at, k, slabs):
        take = self.right if side > 0 else self.left
        tail = roll(take(at + 8 * slabs), -(4 + 8 * k), 1)
        return jnp.concatenate([take(at + 8 * k), tail], axis=1)


def offsets(slabs):
    part = 8 * slabs + 8
    ocean = 3 * part
    extra = ocean + 8 * ((UNITS + 1) // 2)
    more = extra + 16
    return part, ocean, extra, more


def payload_rows(slabs, kind):
    part, _, _, more = offsets(slabs)
    return {
        "first": more + part + 8 * ((FLOOR_UNITS + TILES + 1) // 2),
        "usual": more,
        "last": more + 8 * (UNITS + FLOOR_UNITS),
    }[kind]


def finish(out, slabs, motion, stress, buoyancy, ocean, floor, mean_row, kind):
    part, ocean_at, extra_at, more_at = offsets(slabs)
    low = iota((8, LANES), 0) < 4

    def get(ref, field, row):
        return lambda k: ref[field, row, 8 * k : 8 * k + 8, :]

    def rate(row, k):
        return SOLID_STEP * buoyancy[0, row, 8 * k : 8 * k + 8, :]

    def sum_x(k):
        xx, xy, xz = (get(stress, f, 1) for f in (0, 3, 4))
        mid = xy(k)
        force = (mid - prev_lane(mid)) + (xz(k) - below(xz, k)) - xx(k)
        return get(motion, 0, 1)(k) + rate(1, k) * force

    def sum_y(k):
        xy, yy, yz = (get(stress, f, 0) for f in (3, 1, 5))
        mid = yy(k)
        force = xy(k) + (next_lane(mid) - mid) + (yz(k) - below(yz, k))
        return get(motion, 1, 0)(k) + rate(0, k) * force

    def sum_z(k):
        xz, yz, zz = (get(stress, f, 0) for f in (4, 5, 2))
        mid = yz(k)
        force = xz(k) + (mid - prev_lane(mid)) + (above(zz, k, slabs) - zz(k))
        return get(motion, 2, 0)(k) + rate(0, k) * force

    def kept(compute, field, row):
        def get_and_keep(k):
            value = compute(k)
            motion[field, row, 8 * k : 8 * k + 8, :] = value
            return value

        return get_and_keep

    (spread,) = upsampled([motion[2, 0, 0:1, :]])
    out.put_solid(0, slabs, kept(sum_x, 0, 1), kept(sum_y, 1, 0))
    out.put_solid(part, slabs, get(stress, 3, 1), kept(sum_z, 2, 0))
    out.put_solid(2 * part, slabs, get(stress, 4, 1), get(stress, 0, 0))
    for t in range(TILES):
        ocean[0, t, 8:16, :] = (
            ocean[0, t, 8:16, :] + UPLIFT_GAIN * floor[1, t, 8:16, :] * spread[t : t + 1]
        )

    def units(ref, fields):
        pairs = [(f, t) for f in range(fields) for t in range(TILES)]
        return [(ref[f, t, 0:8, :], ref[f, t, 8:16, :]) for f, t in pairs]

    out.put_halves(ocean_at, units(ocean, 3))
    top = motion[2, 1, 0:8, :]
    mean_row = jnp.zeros((8, 256), jnp.float32) if mean_row is None else mean_row
    mean_row = jnp.broadcast_to(mean_row, (8, 256))
    for i in range(2):
        lanes = slice(LANES * i, LANES * i + LANES)
        out.put(extra_at + 8 * i, top[:, lanes], mean_row[:, lanes])
    if kind == "first":
        out.put_solid(more_at, slabs, get(buoyancy, 0, 1), get(buoyancy, 0, 0))
        faces = []
        for t in range(TILES):
            wet = floor[1, t, :, :]
            faces.append(((wet * roll(wet, -1, 0))[0:8], wet[8:16]))
        out.put_halves(more_at + part, units(floor, 2) + faces)
    if kind == "last":
        for i, (lower, upper) in enumerate(units(ocean, 3) + units(floor, 2)):
            value = jnp.where(low, upper, lower)
            out.put(more_at + 8 * i, value, value)


def pack_y_kernel(
    motion, stress, buoyancy, first, shear, surface, momentum, depth, wet, one, two
):
    even = lax.rem(lax.axis_index("gy"), 2) == 0
    out = Sender(even, one, two)
    slabs = motion.shape[2] // 8
    lane = iota((8, LANES), 1)
    fields = [(motion, f) for f in range(3)] + [(stress, f) for f in range(6)]
    fields += [(buoyancy, None), (first, None), (shear, None)]
    count, at = 0, 0
    right = left = jnp.zeros((8, LANES), jnp.float32)
    for ref, f in fields:
        for row in range(2):
            for k in range(slabs):
                z = slice(8 * k, 8 * k + 8)
                value = ref[row, z, :] if f is None else ref[f, row, z, :]
                here = lane >> 2 == count
                right = jnp.where(here, roll(value, 4 * count + 4, 1), right)
                left = jnp.where(here, roll(value, 4 * count, 1), left)
                count += 1
                if count == 32:
                    out.put(at, right, left)
                    count, at = 0, at + 8
    if count:
        out.put(at, right, left)
        count, at = 0, at + 8
    width = surface.shape[1]
    for ref, f in ((surface, None), (momentum, 0), (momentum, 1), (depth, None), (wet, None)):
        for group in range(2):
            rows = slice(8 * group, 8 * group + 8)
            ends = []
            for lanes in (slice(0, LANES), slice(width - LANES, width)):
                value = ref[rows, lanes] if f is None else ref[f, rows, lanes]
                ends.append(value.astype(jnp.float32))
            here = lane >> 5 == count
            right = jnp.where(here, roll(ends[1], 32 * count + 32, 1), right)
            left = jnp.where(here, roll(ends[0], 32 * count, 1), left)
            count += 1
            if count == 4:
                out.put(at, right, left)
                count, at = 0, at + 8
    if count:
        out.put(at, right, left)


def pack_y_rows(slabs):
    return 8 * (-(-24 * slabs // 32) + 3)


def start_kernel(
    motion, stress, buoyancy, first, shear, surface, momentum, depth, wet, one, two,
    motion_out, stress_out, solid_out, ocean_out, floor_out, send_one, send_two,
):
    inbox = Receiver(lax.rem(lax.axis_index("gy"), 2) == 0, one, two)
    slabs = motion.shape[2] // 8
    lane = iota((8, LANES), 1)
    fields = [(motion, f, motion_out, f) for f in range(3)]
    fields += [(stress, f, stress_out, f) for f in range(6)]
    fields += [(ref, None, solid_out, f) for f, ref in enumerate((buoyancy, first, shear))]
    count, at = 0, 0
    for ref, f, target, g in fields:
        for row in range(2):
            for k in range(slabs):
                z = slice(8 * k, 8 * k + 8)
                value = ref[row, z, :] if f is None else ref[f, row, z, :]
                if count == 0:
                    packed = inbox.right(at), inbox.left(at)
                after = roll(packed[0], -4 * count, 1)
                before = roll(packed[1], 124 - 4 * count, 1)
                halo = jnp.where(lane < 4, after, jnp.where(lane >= 124, before, 0.0))
                target[g, row, z, 0:LANES] = value
                target[g, row, z, LANES : 2 * LANES] = halo
                count += 1
                if count == 32:
                    count, at = 0, at + 8
    if count:
        count, at = 0, at + 8
    targets = ((surface, None), (momentum, 0), (momentum, 1), (depth, None), (wet, None))
    for i, (ref, f) in enumerate(targets):
        for group in range(2):
            rows = slice(8 * group, 8 * group + 8)
            if count == 0:
                packed = inbox.right(at), inbox.left(at)
            after = roll(packed[0], -32 * count, 1)
            before = roll(packed[1], 96 - 32 * count, 1)
            halo = jnp.where(lane < 32, after, jnp.where(lane >= 96, before, 0.0))
            for t in range(TILES):
                if t == TILES - 1:
                    value = halo
                else:
                    lanes = slice(LANES * t, LANES * t + LANES)
                    value = ref[rows, lanes] if f is None else ref[f, rows, lanes]
                    value = value.astype(jnp.float32)
                if i < 3:
                    ocean_out[i, t, rows, :] = value
                else:
                    floor_out[i - 3, t, rows, :] = value
            count += 1
            if count == 4:
                count, at = 0, at + 8
    out = Sender(lax.rem(lax.axis_index("gx"), 2) == 0, send_one, send_two)
    finish(out, slabs, motion_out, stress_out, solid_out, ocean_out, floor_out, None, "first")


PAD = 8


class Shifts:
    def __init__(self, tile, by):
        self.tile, self.by, self.rolled = tile, by, {}

    def rotated(self, t):
        if t not in self.rolled:
            self.rolled[t] = roll(self.tile(t), self.by, 1)
        return self.rolled[t]

    def at(self, t):
        lane = iota((8, LANES), 1)
        other, mine = self.rotated((t - self.by) % TILES), self.rotated(t)
        return jnp.where(lane == (0 if self.by > 0 else LANES - 1), other, mine)


def coefficients(coef, face, depth, after):
    groups = coef.shape[2] // 8
    for t in range(TILES):
        for g in range(groups):
            at = PAD + 8 * g
            wet = face[0, t, at : at + 8, :]
            coef[7, t, 8 * g : 8 * g + 8, :] = wet
            coef[0, t, 8 * g : 8 * g + 8, :] = WAVE_STEP * wet
    for direction in range(2):
        for g in range(groups):
            at = PAD + 8 * g
            wets = Shifts(lambda t: coef[7, t, 8 * g : 8 * g + 8, :], -1)
            depths = Shifts(lambda t: depth[t, at : at + 8, :], -1)
            for t in range(TILES):
                wet = wets.tile(t)
                here = depths.tile(t)
                if direction == 0:
                    beside = face[0, t, at + 1 : at + 9, :]
                    deep = depth[t, at + 1 : at + 9, :]
                else:
                    beside, deep = wets.at(t), depths.at(t)
                face[1, t, at : at + 8, :] = wet * beside
                coef[3 + 3 * direction, t, 8 * g : 8 * g + 8, :] = here + deep
        if direction == 0 and after is not None:
            for t in range(TILES):
                face[1, t, PAD + 20 : PAD + 28, :] = after(t)
        for g in range(groups):
            at = PAD + 8 * g
            ahead = Shifts(lambda t: face[1, t, at : at + 8, :], -1)
            behind = Shifts(ahead.tile, 1)
            for t in range(TILES):
                own = ahead.tile(t)
                total = face[1, t, at - 1 : at + 7, :] + face[1, t, at + 1 : at + 9, :]
                total = total + ahead.at(t) + behind.at(t)
                rows = slice(8 * g, 8 * g + 8)
                coef[1 + 3 * direction, t, rows, :] = VISCOSITY * own
                coef[2 + 3 * direction, t, rows, :] = own - VISCOSITY * own * total


def ocean_part(
    inbox, base, slabs, motion, ocean, floor, wide, first, coef, height, flow, side, row_left
):
    part, ocean_at, _, more_at = offsets(slabs)
    low = iota((8, LANES), 0) < 4
    groups = 4 if wide else 3

    def place(target, t, own, near, top, far):
        target[t, PAD - 4 : PAD + 4, :] = top
        target[t, PAD + 4 : PAD + 20, :] = own
        if wide:
            near = jnp.where(low, near, far)
            target[t, PAD + 28 : PAD + 36, :] = far
        target[t, PAD + 20 : PAD + 28, :] = near

    if first or wide:
        for t in range(TILES):
            for f, target in ((1, flow.at[0, 0]), (0, height)):
                near, top = base.halves(more_at + part, f * TILES + t)
                far = inbox.right(more_at + 8 * (UNITS + f * TILES + t)) if wide else None
                place(target, t, floor[f, t, :, :], near, top, far)
        after = lambda t: base.halves(more_at + part, 2 * TILES + t)[0]
        coefficients(coef, flow.at[0], height, None if wide else after)
    spread_left, spread_last = upsampled([row_left, motion[2, 1, 0:1, :]])
    for t in range(TILES):
        for f in range(3):
            near, top = inbox.halves(ocean_at, f * TILES + t)
            far = inbox.right(more_at + 8 * (f * TILES + t)) if wide else None
            target = height if f == 0 else flow.at[0, f - 1]
            place(target, t, ocean[f, t, :, :], near, top, far)
        for g in range(groups):
            spread = spread_left if g < 2 else spread_last
            lift = UPLIFT_GAIN * coef[7, t, 8 * g : 8 * g + 8, :] * spread[t : t + 1]
            lift = jnp.where(low == (g % 2 == 1), lift, 0.0)
            at = PAD + 8 * g
            height[t, at : at + 8, :] = height[t, at : at + 8, :] + lift
    for step in range(NSUB):
        old, new = step % 2, (step + 1) % 2
        for g in range(groups):
            at, rows = PAD + 8 * g, slice(8 * g, 8 * g + 8)
            n_behind = Shifts(lambda t: flow[old, 1, t, at : at + 8, :], 1)
            for t in range(TILES):
                m, n = flow[old, 0, t, at : at + 8, :], n_behind.tile(t)
                west = n_behind.at(t)
                if not (first and step == 0):
                    side[t, rows, :] = west
                spill = (m - flow[old, 0, t, at - 1 : at + 7, :]) + (n - west)
                height[t, at : at + 8, :] = height[t, at : at + 8, :] - coef[0, t, rows, :] * spill
        if first and step == 0:
            for t in range(TILES):
                for g in range(groups):
                    at, rows = PAD + 8 * g, slice(8 * g, 8 * g + 8)
                    for d in range(2):
                        wet = jnp.where(coef[1 + 3 * d, t, rows, :] > 0.0, 1.0, 0.0)
                        flow[old, d, t, at : at + 8, :] = wet * flow[old, d, t, at : at + 8, :]
        for g in range(groups):
            at, rows = PAD + 8 * g, slice(8 * g, 8 * g + 8)
            h_ahead = Shifts(lambda t: height[t, at : at + 8, :], -1)
            ahead = [Shifts(lambda t, d=d: flow[old, d, t, at : at + 8, :], -1) for d in range(2)]
            m_behind = Shifts(ahead[0].tile, 1)
            n_behind = Shifts(ahead[1].tile, 1)
            for t in range(TILES):
                h = height[t, at : at + 8, :]
                sides = [height[t, at + 1 : at + 9, :], h_ahead.at(t)]
                for d in range(2):
                    q = flow[old, d, t, at : at + 8, :]
                    around = flow[old, d, t, at - 1 : at + 7, :] + flow[old, d, t, at + 1 : at + 9, :]
                    around = around + ahead[d].at(t)
                    if d == 0:
                        around = around + m_behind.at(t)
                    elif first and step == 0:
                        around = around + n_behind.at(t)
                    else:
                        around = around + side[t, rows, :]
                    c = 1 + 3 * d
                    slope = (coef[c + 2, t, rows, :] + h + sides[d]) * (sides[d] - h)
                    value = coef[c + 1, t, rows, :] * q + coef[c, t, rows, :] * (around - slope)
                    flow[new, d, t, at : at + 8, :] = value


def step_kernel(last, is_first, edge, *refs):
    refs = list(refs)

    def take(count):
        taken = refs[:count]
        del refs[:count]
        return taken

    base_one, base_two = take(2)
    one, two = (base_one, base_two) if is_first else take(2)
    motion, stress, solid, ocean, floor = take(5)
    ready = not (is_first or last)
    if ready:
        (coef,) = take(1)
    if last:
        motion_out, stress_out, surface_out, momentum_out = take(4)
    else:
        motion_out, stress_out, ocean_out, send_one, send_two = take(5)
    if not ready:
        (coef,) = take(1)
    height, flow, side, speed = take(4)
    slabs = motion.shape[2] // 8
    part, _, extra_at, more_at = offsets(slabs)
    even = lax.rem(lax.axis_index("gx"), 2) == 0
    base = Receiver(even, base_one, base_two)
    inbox = Receiver(even, one, two)

    def extra_row(take):
        return jnp.concatenate([take(extra_at)[0:1], take(extra_at + 8)[0:1]], axis=1)

    row_left = extra_row(inbox.left)
    loaded = None if is_first else -LOAD_GAIN * extra_row(inbox.right)
    ocean_part(
        inbox, base, slabs, motion, ocean, floor, last, is_first, coef, height, flow, side, row_left
    )
    blocks = 3 if last else 2
    sums = [[] for _ in range(blocks)]
    rows = slice(PAD + 4, PAD + 20)
    for t in range(TILES):
        for b in range(blocks):
            at = 8 * b + 4
            wet = coef[7, t, at : at + 8, :]
            h = height[t, PAD + at : PAD + at + 8, :]
            sums[b].append(jnp.sum(wet * h, axis=0, keepdims=True))
        if last:
            if t < TILES - 1:
                lanes = slice(LANES * t, LANES * t + LANES)
                surface_out[:, lanes] = height[t, rows, :]
                for d in range(2):
                    momentum_out[d, :, lanes] = flow[NSUB % 2, d, t, rows, :]
        else:
            ocean_out[0, t] = height[t, rows, :]
            for d in range(2):
                ocean_out[1 + d, t] = flow[NSUB % 2, d, t, rows, :]
    means = block_means(sums)

    def old(f, row):
        def get(k):
            value = stress[f, row, 8 * k : 8 * k + 8, :]
            if (f, row, k) == (2, 1, 0) and loaded is not None:
                value = jnp.where(iota(value.shape, 0) == 0, loaded, value)
            return value

        return get

    def new(f, row):
        return lambda k: speed[f, row, 8 * k : 8 * k + 8, :]

    for k in range(slabs):
        z = slice(8 * k, 8 * k + 8)
        xx = [stress[0, 0, z, :], stress[0, 1, z, :], inbox.solid(1, 2 * part, k, slabs)]
        xy = [inbox.solid(-1, part, k, slabs), stress[3, 0, z, :], stress[3, 1, z, :]]
        xz = [inbox.solid(-1, 2 * part, k, slabs), stress[4, 0, z, :], stress[4, 1, z, :]]
        rate_left = SOLID_STEP * base.solid(-1, more_at, k, slabs)
        rate_right = SOLID_STEP * base.solid(1, more_at, k, slabs)
        speed[0, 2, z, :] = inbox.solid(-1, 0, k, slabs) + rate_left * xx[0]
        speed[1, 2, z, :] = inbox.solid(1, 0, k, slabs) - rate_right * xy[2]
        speed[2, 2, z, :] = inbox.solid(1, part, k, slabs) - rate_right * xz[2]
        rates = [SOLID_STEP * solid[0, row, z, :] for row in range(2)]
        whole_x = (xx[1] - xx[0]) + (xy[1] - prev_lane(xy[1])) + (xz[1] - below(old(4, 0), k))
        yy, zz, yz = stress[1, 1, z, :], old(2, 1), stress[5, 1, z, :]
        whole_y = (xy[2] - xy[1]) + (next_lane(yy) - yy) + (yz - below(old(5, 1), k))
        whole_z = (xz[2] - xz[1]) + (yz - prev_lane(yz)) + (above(zz, k, slabs) - zz(k))
        forces = {
            (0, 0): whole_x, (0, 1): xx[2],
            (1, 0): -xy[0], (1, 1): whole_y,
            (2, 0): -xz[0], (2, 1): whole_z,
        }
        for (f, row), force in forces.items():
            value = motion[f, row, z, :] + rates[row] * force
            speed[f, row, z, :] = value
            motion_out[f, row, z, :] = value[:, :LANES] if last else value
    width = LANES if last else 2 * LANES
    for k in range(slabs):
        z = slice(8 * k, 8 * k + 8)
        x_of = [speed[0, 2, z, :], speed[0, 0, z, :], speed[0, 1, z, :]]
        y_of = [speed[1, 0, z, :], speed[1, 1, z, :], speed[1, 2, z, :]]
        z_of = [speed[2, 0, z, :], speed[2, 1, z, :], speed[2, 2, z, :]]
        for row in range(2):
            vx, vy, vz = x_of[row + 1], y_of[row], z_of[row]
            strain_x = vx - x_of[row]
            strain_y = vy - prev_lane(vy)
            strain_z = vz - below(new(2, row), k)
            shear = SOLID_STEP * solid[2, row, z, :]
            lame = SOLID_STEP * solid[1, row, z, :]
            common = lame * (strain_x + strain_y + strain_z)
            twice = shear + shear
            rates = [common + twice * strain for strain in (strain_x, strain_y, strain_z)]
            rates.append(shear * ((next_lane(vx) - vx) + (y_of[row + 1] - vy)))
            rates.append(shear * ((above(new(0, row), k, slabs) - vx) + (z_of[row + 1] - vz)))
            rates.append(shear * ((above(new(1, row), k, slabs) - vy) + (next_lane(vz) - vz)))
            for f in range(6):
                value = stress[f, row, z, :] + rates[f]
                stress_out[f, row, z, :] = value[:, :width]
    stress_out[2, 0, 0:1, :] = -LOAD_GAIN * means[1][:, :width]
    if last:
        stress_out[2, 1, 0:1, :] = -LOAD_GAIN * means[2][:, :width]
        return
    out = Sender(even, send_one, send_two)
    next_kind = "last" if edge else "usual"
    finish(out, slabs, motion_out, stress_out, solid, ocean_out, floor, means[0], next_kind)


def swap(size, start):
    pairs = []
    for i in range(start, size - 1, 2):
        pairs += [(i, i + 1), (i + 1, i)]
    return pairs


def exchanged(first, second, axis):
    size = lax.axis_size(axis)
    return (
        lax.ppermute(first, axis, swap(size, 0)),
        lax.ppermute(second, axis, swap(size, 1)),
    )


def body(motion, stress, buoyancy, lame_first, lame_shear, surface, momentum, bathymetry, wet_mask):
    depth_cells = motion.shape[2]
    slabs = depth_cells // 8
    f32 = jnp.float32

    def array(*shape):
        return jax.ShapeDtypeStruct(shape, f32)

    def call(kernel, outs, args, scratch=(), grant=VMEM_LIMIT):
        specs = [pl.BlockSpec(memory_space=pltpu.VMEM)] * len(args)
        return pl.pallas_call(
            kernel,
            out_shape=outs,
            in_specs=specs,
            out_specs=tuple(pl.BlockSpec(memory_space=pltpu.VMEM) for _ in outs),
            scratch_shapes=list(scratch),
            compiler_params=pltpu.CompilerParams(vmem_limit_bytes=grant),
            interpret=INTERPRET,
        )(*args)

    own = (
        motion, stress, buoyancy, lame_first, lame_shear, surface, momentum, bathymetry, wet_mask,
    )
    state = (array(3, 2, depth_cells, 256), array(6, 2, depth_cells, 256))
    wide = (
        *state,
        array(3, 2, depth_cells, 256),
        array(3, TILES, 16, LANES),
        array(2, TILES, 16, LANES),
    )
    packed = (array(pack_y_rows(slabs), LANES),) * 2
    received = exchanged(*call(pack_y_kernel, packed, own, grant=LOADER_LIMIT), "gy")
    packed = (array(payload_rows(slabs, "first"), LANES),) * 2
    motion, stress, solid, ocean, floor, *send = call(
        start_kernel, (*wide, *packed), (*own, *received)
    )
    base = coef = None
    for step in range(STEPS):
        received = exchanged(*send, "gx")
        first, last, edge = step == 0, step == STEPS - 1, step == STEPS - 2
        height = 32 if last else 24
        table = (8, TILES, height, LANES)
        padded = height + 2 * PAD
        scratch = [
            pltpu.VMEM((TILES, padded, LANES), f32),
            pltpu.VMEM((2, 2, TILES, padded, LANES), f32),
            pltpu.VMEM((TILES, height, LANES), f32),
            pltpu.VMEM((3, 3, depth_cells, 256), f32),
        ]
        rows = payload_rows(slabs, "last" if edge else "usual")
        outs = (*state, array(3, TILES, 16, LANES), array(rows, LANES), array(rows, LANES))
        fixed = (motion, stress, solid, ocean, floor)
        if first:
            base = received
            inputs = (*base, *fixed)
            outs = (*outs, array(*table))
        elif last:
            inputs = (*base, *received, *fixed)
            scratch = [pltpu.VMEM(table, f32), *scratch]
            outs = (
                array(3, 2, depth_cells, LANES),
                array(6, 2, depth_cells, LANES),
                array(16, 8 * LANES),
                array(2, 16, 8 * LANES),
            )
        else:
            inputs = (*base, *received, *fixed, coef)
        kernel = functools.partial(step_kernel, last, first, edge)
        results = call(kernel, outs, inputs, scratch)
        if first:
            coef = results[-1]
        if not last:
            motion, stress, ocean, *send = results[:5]
    return results


def solution(mesh):
    return jax.shard_map(
        body,
        mesh=mesh,
        in_specs=(
            P(None, "gx", None, "gy"),
            P(None, "gx", None, "gy"),
            P("gx", None, "gy"),
            P("gx", None, "gy"),
            P("gx", None, "gy"),
            P("gx", "gy"),
            P(None, "gx", "gy"),
            P("gx", "gy"),
            P("gx", "gy"),
        ),
        out_specs=(
            P(None, "gx", None, "gy"),
            P(None, "gx", None, "gy"),
            P("gx", "gy"),
            P(None, "gx", "gy"),
        ),
        check_vma=False,
    )
```
